512 devices in a mesh: seq: 32 (over x, z), head: 16 (over y, core).
Axes of the slice: x: 4, y: 8, z: 8, core: 2. Of those that a mesh axis runs over, the one named last changes fastest.
Arguments:
- xs: bfloat16 [49152, 5120], P('seq', 'head'), may hold values from -6 to 6
- dxs: bfloat16 [49152, 5120], P('seq', 'head'), may hold values from -6 to 6
- zgate: bfloat16 [49152, 5120], P('seq', 'head'), may hold values from -6 to 6
- bmat: bfloat16 [49152, 128], P('seq'), may hold values from -1 to 1
- cmat: bfloat16 [49152, 128], P('seq'), may hold values from -1 to 1
- dt_raw: float32 [80, 49152], P('head', 'seq'), may hold values from -3 to 3
- dt_bias: float32 [80], P('head'), may hold values from -1 to 1
- a_rate: float32 [80], P('head'), may hold values from 0 to 1, as said below
- d_skip: float32 [80], P('head'), may hold values from 0.5 to 2
- gain: float32 [5120], replicated, may hold values from 0.5 to 1.5
- traj_ids: int32 [192], P('seq'), may hold values from 0 to 9, as said below
Outputs:
- normed: bfloat16 [49152, 5120], P(('seq', 'head'))
- normed_tan: bfloat16 [49152, 5120], P(('seq', 'head'))
The draws below stay inside these ranges and needn't reach their ends.
Inputs may be any that keep to these rules, and one draw needn't show every extreme that they name: `traj_ids`: never falling from one block to the next; trajectory 0 spans exactly the first 96 blocks, trajectory 1 the next 6 blocks or more, every other trajectory one block or more. `a_rate`: positive.
All inputs are finite; a program needn't handle non-finite values.
Results may differ from the reference program's by a relative error of at most 0.0057.
Values may be sent and summed in bfloat16 or wider, within the bound.
No kernel may reach another device: no remote copies, remote signals or barrier semaphores. Data moves between devices by JAX's collectives and lax.ppermute only.
A program may use at most 128 MiB of HBM per device.

```python
import jax
import jax.numpy as jnp
from jax import lax

P_SIZE = 64
N = 128
Q = 256
BLK_DEV = 6
HEADS = 80
INNER = 5120
TOKENS = 49152
NBLOCKS = 192
TRAJS = 10


def draw_a_rate(key, part):
    pick_key, spread_key = jax.random.split(key)
    slow_share = 0.5
    slow_flag = jax.random.uniform(pick_key, (HEADS,), jnp.float32) < slow_share
    position = jax.random.uniform(spread_key, (HEADS,), jnp.float32)
    slow_low = jnp.log(jnp.float32(0.2 / TOKENS))
    slow_high = jnp.log(jnp.float32(2.0 / TOKENS))
    boundary = jnp.log(jnp.float32(60.0 / TOKENS))
    slow_rate = jnp.exp(slow_low + (slow_high - slow_low) * position)
    fast_rate = jnp.exp(boundary * (1.0 - position))
    return jnp.where(slow_flag, slow_rate, fast_rate).astype(jnp.float32)


def draw_traj_ids(key, part):
    first_span = NBLOCKS // 2
    rest_blocks = NBLOCKS - first_span
    cut_count = TRAJS - 2
    pool = rest_blocks - BLK_DEV
    cuts = jax.random.permutation(jax.random.fold_in(key, 7), jnp.arange(pool, dtype=jnp.int32))[:cut_count] + BLK_DEV
    marks = jnp.zeros((rest_blocks,), jnp.int32).at[cuts].set(1)
    rest_ids = jnp.cumsum(marks).astype(jnp.int32) + 1
    return jnp.concatenate([jnp.zeros((first_span,), jnp.int32), rest_ids]).astype(jnp.int32)


def level_of(stream_key, extent, pieces, least, top_value):
    loudness = 1.0
    for axis_at, parts in pieces:
        steps = jax.random.uniform(jax.random.fold_in(jax.random.fold_in(stream_key, 6), axis_at), (parts,), jnp.float32, least / len(pieces), top_value / len(pieces))
        loudness = loudness * jnp.repeat(jnp.exp(steps), extent[axis_at] // parts).reshape((-1,) + (1,) * (len(extent) - 1 - axis_at))
    return loudness


def gaussian(key, shape, spread, reach, cuts=(), kind=jnp.bfloat16):
    entries = jax.random.normal(key, shape, jnp.float32) * spread
    if len(cuts) > 0:
        entries = level_of(key, shape, cuts, -0.22, 0.18) * entries
    return jnp.clip(entries, min=-reach, max=reach).astype(kind)


def setup_inputs(seed: int = 0) -> dict:
    streams_of = jax.random.split(jax.random.key(seed), 12)
    xs = gaussian(streams_of[0], (TOKENS, INNER), 1.0, 6.0, ((0, 32), (1, 16)))
    dxs = gaussian(streams_of[1], (TOKENS, INNER), 1.0, 6.0, ((0, 32), (1, 16)))
    zgate = gaussian(streams_of[2], (TOKENS, INNER), 1.0, 6.0, ((0, 32), (1, 16)))
    bmat = gaussian(streams_of[3], (TOKENS, N), 0.15, 1.0, ((0, 32),))
    cmat = gaussian(streams_of[4], (TOKENS, N), 0.15, 1.0, ((0, 32),))
    dt_raw = gaussian(streams_of[5], (HEADS, TOKENS), 0.5, 3.0, ((0, 16), (1, 32)), jnp.float32)
    dt_bias = jnp.clip(jax.random.uniform(streams_of[6], (HEADS,), jnp.float32, -1.0, 1.0) * level_of(streams_of[6], (HEADS,), ((0, 16),), -0.4, 0.0), -1.0, 1.0)
    a_rate = draw_a_rate(jax.random.fold_in(streams_of[11], 71), 0)
    d_skip = jnp.clip(0.5 + 1.5 * jax.random.uniform(streams_of[8], (HEADS,), jnp.float32) ** level_of(streams_of[8], (HEADS,), ((0, 16),), -0.2, 0.2), 0.5, 2.0)
    gain = jnp.clip(1.0 + 0.1 * jax.random.normal(streams_of[9], (INNER,), jnp.float32), 0.5, 1.5)
    traj_ids = draw_traj_ids(jax.random.fold_in(streams_of[11], 71), 0)
    return {"xs": xs, "dxs": dxs, "zgate": zgate, "bmat": bmat, "cmat": cmat, "dt_raw": dt_raw, "dt_bias": dt_bias, "a_rate": a_rate, "d_skip": d_skip, "gain": gain, "traj_ids": traj_ids}


def block_terms(joined, b_block, c_block, step_block, log_block, state_in):
    token_count = joined.shape[0]
    scores = jnp.dot(c_block, b_block.T, preferred_element_type=jnp.float32)
    places = jnp.arange(token_count)
    causal_mask = places[:, None] >= places[None, :]
    log_gap = log_block[:, :, None] - log_block[:, None, :]
    decay_table = jnp.exp(jnp.where(causal_mask[None], log_gap, -jnp.inf))
    weights = (scores[None] * decay_table * step_block[:, None, :]).astype(jnp.bfloat16)
    y_diag = jnp.einsum('hts,shp->thp', weights.astype(jnp.float32), joined.astype(jnp.float32))
    end_log = log_block[:, -1]
    weight_in = step_block * jnp.exp(end_log[:, None] - log_block)
    weighted = (joined.astype(jnp.float32) * weight_in.T[:, :, None]).astype(jnp.bfloat16)
    block_state = jnp.einsum('shp,sn->hpn', weighted.astype(jnp.float32), b_block.astype(jnp.float32))
    y_off = jnp.einsum('tn,hpn->thp', c_block.astype(jnp.float32), state_in, precision=lax.Precision.HIGHEST) * jnp.exp(log_block).T[:, :, None]
    leaving = jnp.exp(end_log)[:, None, None] * state_in + block_state
    return (y_diag + y_off, leaving)

def reference(xs, dxs, zgate, bmat, cmat, dt_raw, dt_bias, a_rate, d_skip, gain, traj_ids):
    step_size = jax.nn.softplus(dt_raw + dt_bias[:, None])
    step_blocks = step_size.reshape(HEADS, NBLOCKS, Q).transpose(1, 0, 2)
    log_blocks = jnp.cumsum(-(step_blocks * a_rate[None, :, None]), axis=-1)
    joined = jnp.concatenate([xs.reshape(NBLOCKS, Q, HEADS, P_SIZE), dxs.reshape(NBLOCKS, Q, HEADS, P_SIZE)], axis=-1)
    keep_flags = jnp.concatenate([jnp.zeros((1,), jnp.float32), (traj_ids[1:] == traj_ids[:-1]).astype(jnp.float32)])

    def advance(carried, item):
        joined_block, b_block, c_block, step_block, log_block, keep_flag = item
        state_in = keep_flag * carried
        y_block, leaving = block_terms(joined_block, b_block, c_block, step_block, log_block, state_in)
        return (leaving, y_block)
    zero_state = jnp.zeros((HEADS, 2 * P_SIZE, N), jnp.float32)
    items = (joined, bmat.reshape(NBLOCKS, Q, N), cmat.reshape(NBLOCKS, Q, N), step_blocks, log_blocks, keep_flags)
    _, y_blocks = lax.scan(advance, zero_state, items)
    y_total = y_blocks + joined.astype(jnp.float32) * d_skip[None, None, :, None]
    y_joined = y_total.reshape(TOKENS, HEADS, 2 * P_SIZE).astype(jnp.bfloat16)
    y_main = y_joined[:, :, :P_SIZE].reshape(TOKENS, INNER)
    y_tan = y_joined[:, :, P_SIZE:].reshape(TOKENS, INNER)
    gate_value = jax.nn.silu(zgate.astype(jnp.float32))
    gated = y_main.astype(jnp.float32) * gate_value
    gated_tan = y_tan.astype(jnp.float32) * gate_value
    mean_square = lax.optimization_barrier(jnp.mean(gated * gated, axis=-1, keepdims=True))
    mean_cross = lax.optimization_barrier(jnp.mean(gated * gated_tan, axis=-1, keepdims=True))
    inv_rms = lax.rsqrt(mean_square + 1e-05)
    normed = (gain * gated * inv_rms).astype(jnp.bfloat16)
    normed_tan = (gain * (gated_tan * inv_rms - gated * inv_rms ** 3 * mean_cross)).astype(jnp.bfloat16)
    return (normed, normed_tan)
```

```python
import functools

import jax
import jax.numpy as jnp
from jax import lax
from jax.experimental import pallas as pl
from jax.experimental.pallas import tpu as pltpu
from jax.sharding import PartitionSpec as P

Q = 256
HALF = 128
LANES = 128
PACK = 8
LOG2E = 1.4426950408889634
VMEM_BYTES = 48 * 1024 * 1024
F32 = jnp.float32
BF16 = jnp.bfloat16


def column_of(values):
    place = lax.broadcasted_iota(jnp.int32, (PACK, 1), 0)
    column = jnp.zeros((PACK, 1), F32)
    for h, value in enumerate(values):
        column = jnp.where(place == h, value, column)
    return column


def by_head(per_head, rows):
    low = lax.broadcasted_iota(jnp.int32, (rows, LANES), 1) < LANES // 2
    first = jnp.where(low, per_head[0], per_head[1])
    second = jnp.where(low, per_head[2], per_head[3])
    last = jnp.broadcast_to(per_head[4], (rows, LANES))
    return [first, first, second, second, last]


def head_tiles(main, tan):
    return [
        main[:, 0:128],
        tan[:, 0:128],
        main[:, 128:256],
        tan[:, 128:256],
        jnp.concatenate([main[:, 256:320], tan[:, 256:320]], axis=1),
    ]


def split_bf16(x, parts):
    pieces = []
    for _ in range(parts):
        piece = x.astype(BF16)
        pieces.append(piece)
        x = x - piece.astype(F32)
    return pieces


def state_kernel(
    heads, blocks, dt_bias, a_rate, traj, xs, dxs, bmat, dt_raw, rows, cols, local_in, fin, send
):
    bias = column_of([dt_bias[h] for h in range(heads)])
    rate = column_of([a_rate[h] * LOG2E for h in range(heads)])
    raw = jnp.concatenate([dt_raw[...], jnp.zeros((PACK - heads, blocks * Q), F32)], axis=0)
    pre = jnp.concatenate([raw[:, c * Q : (c + 1) * Q] for c in range(blocks)], axis=0)
    bias_all = jnp.concatenate([bias] * blocks, axis=0)
    rate_all = jnp.concatenate([rate] * blocks, axis=0)
    pre = pre + bias_all
    step = jnp.maximum(pre, 0.0) + jnp.log1p(jnp.exp(-jnp.abs(pre)))
    upper = (
        lax.broadcasted_iota(jnp.int32, (Q, Q), 0) <= lax.broadcasted_iota(jnp.int32, (Q, Q), 1)
    ).astype(BF16)
    logs = jnp.zeros((blocks * PACK, Q), F32)
    for piece in split_bf16(-(step * rate_all), 3)[::-1]:
        logs = logs + jnp.dot(piece, upper, preferred_element_type=F32)
    shifted = logs - jnp.log2(step)
    rows[...] = shifted
    ends = logs[:, Q - 1 : Q]
    weight_in = jnp.exp2(ends - shifted)
    end_decay = jnp.exp2(ends)

    state = jnp.zeros((LANES, heads * LANES), F32)
    factor = [jnp.ones((1, 1), F32)] * heads
    for c in range(blocks):
        at = slice(c * PACK, (c + 1) * PACK)
        table = jnp.concatenate(
            [weight_in[at], logs[at], jnp.zeros((LANES - 2 * PACK, Q), F32)], axis=0
        ).T
        here = slice(c * Q, (c + 1) * Q)
        cols[here, :] = table
        if c > 0:
            keep = jnp.where(traj[c] == traj[c - 1], 1.0, 0.0)
            state = state * keep
            factor = [f * keep for f in factor]
        local_in[c] = state.astype(BF16)
        fin[c : c + 1, :] = jnp.concatenate(by_head(factor, 1), axis=1)
        scale = by_head([table[:, h : h + 1] for h in range(heads)], Q)
        tiles = head_tiles(xs[here, :], dxs[here, :])
        weighted = jnp.concatenate(
            [(t.astype(F32) * s).astype(BF16) for t, s in zip(tiles, scale)], axis=1
        )
        gained = lax.dot_general(
            bmat[here, :], weighted, (((0,), (0,)), ((), ())), preferred_element_type=F32
        )
        ended = [end_decay[c * PACK + h : c * PACK + h + 1, :] for h in range(heads)]
        state = state * jnp.concatenate(by_head(ended, 1), axis=1) + gained
        factor = [f * e for f, e in zip(factor, ended)]
    fin[blocks:PACK, :] = jnp.zeros((PACK - blocks, heads * LANES), F32)
    lane = lax.broadcasted_iota(jnp.int32, (1, LANES), 1)
    notes = jnp.zeros((1, LANES), F32)
    for h in range(heads):
        rest = factor[h]
        for k in range(3):
            piece = rest.astype(BF16).astype(F32)
            notes = jnp.where(lane == k * heads + h, piece, notes)
            rest = rest - piece
    notes = jnp.where(lane == 3 * heads, traj[0].astype(F32), notes)
    notes = jnp.where(lane == 3 * heads + 1, traj[blocks - 1].astype(F32), notes)
    send[:, : heads * LANES] = state.astype(BF16)
    send[:, heads * LANES :] = jnp.broadcast_to(notes, (LANES, LANES)).astype(BF16)


def scan_kernel(heads, count, got, back, hold):
    width = heads * LANES
    everything = got[...].astype(F32)
    carried = jnp.zeros((PACK, width), F32)
    last_id = None
    for s in range(count):
        at = slice(s * PACK, (s + 1) * PACK)
        notes = everything[at, width:]
        factor = []
        for h in range(heads):
            total = notes[:, h : h + 1]
            for k in range(1, 3):
                total = total + notes[:, k * heads + h : k * heads + h + 1]
            factor.append(total)
        first_id = notes[:, 3 * heads : 3 * heads + 1]
        if s > 0:
            carried = jnp.where(first_id == last_id, carried, 0.0)
        hold[at, :] = carried
        last_id = notes[:, 3 * heads + 1 : 3 * heads + 2]
        carried = jnp.concatenate(by_head(factor, PACK), axis=1) * carried + everything[at, :width]
    back[...] = hold[...].astype(BF16)


def diagonal_kernel(heads, d_skip, xs, dxs, bmat, cmat, rows, cols, local_in, out):
    scores = lax.dot_general(
        cmat[...], bmat[...], (((1,), (1,)), ((), ())), preferred_element_type=F32
    )
    causal = lax.broadcasted_iota(jnp.int32, (HALF, HALF), 0) >= lax.broadcasted_iota(
        jnp.int32, (HALF, HALF), 1
    )
    tiles = head_tiles(xs[...], dxs[...])
    operands = [
        jnp.concatenate(tiles[0:2], axis=1),
        jnp.concatenate(tiles[2:4], axis=1),
        tiles[4],
    ]
    low = lax.broadcasted_iota(jnp.int32, (Q, LANES), 1) < LANES // 2
    sums = []
    for h in range(heads):
        log_t = cols[:, PACK + h : PACK + h + 1]
        log_s = rows[h : h + 1, :]
        near = jnp.where(
            causal, scores[:HALF, :HALF] * jnp.exp2(log_t[:HALF] - log_s[:, :HALF]), 0.0
        )
        far = scores[HALF:, :HALF] * jnp.exp2(log_t[HALF:] - log_s[:, :HALF])
        last = jnp.where(
            causal, scores[HALF:, HALF:] * jnp.exp2(log_t[HALF:] - log_s[:, HALF:]), 0.0
        )
        operand = operands[h // 2]
        top = jnp.dot(near.astype(BF16), operand[:HALF], preferred_element_type=F32)
        low_rows = jnp.concatenate([far, last], axis=1).astype(BF16)
        bottom = jnp.dot(low_rows, operand, preferred_element_type=F32)
        sums.append(jnp.concatenate([top, bottom], axis=0))
    diagonal = []
    for pair in range(heads // 2):
        left, right = sums[2 * pair], sums[2 * pair + 1]
        diagonal.append(jnp.where(low, left[:, :LANES], right[:, :LANES]))
        diagonal.append(jnp.where(low, left[:, LANES:], right[:, LANES:]))
    diagonal.append(sums[heads - 1])
    carried = jnp.dot(cmat[...], local_in[0], preferred_element_type=F32)
    decay = by_head([jnp.exp2(cols[:, PACK + h : PACK + h + 1]) for h in range(heads)], Q)
    skip = by_head([d_skip[h] for h in range(heads)], 1)
    for i in range(heads):
        at = slice(i * LANES, (i + 1) * LANES)
        out[:, at] = (
            diagonal[i] + carried[:, at] * decay[i] + tiles[i].astype(F32) * skip[i]
        )


def gate_kernel(heads, y_local, zgate, cmat, cols, fin, incoming, out):
    block = pl.program_id(0)
    carried = jnp.dot(cmat[...], incoming[...], preferred_element_type=F32)
    decay = by_head([jnp.exp2(cols[:, PACK + h : PACK + h + 1]) for h in range(heads)], Q)
    through = fin[pl.ds(block, 1), :]
    gates = head_tiles(zgate[...], zgate[...])
    for i in range(heads):
        at = slice(i * LANES, (i + 1) * LANES)
        gate = gates[i].astype(F32)
        y = y_local[:, at] + carried[:, at] * (decay[i] * through[:, at])
        out[:, at] = (y * (gate / (1.0 + jnp.exp(-gate)))).astype(BF16)


def norm_kernel(heads, sources, total_width, gathered, gain, normed, normed_tan):
    main_parts, tan_parts = [], []
    half = LANES // 2
    for s in range(sources):
        tiles = [
            gathered[s, :, i * LANES : (i + 1) * LANES].astype(F32) for i in range(heads)
        ]
        main_parts += [tiles[0], tiles[2], tiles[4][:, :half]]
        tan_parts += [tiles[1], tiles[3], tiles[4][:, half:]]
    width = heads * half
    mains, tans = [], []
    for s in range(0, sources, 2):
        mains.append(jnp.concatenate(main_parts[3 * s : 3 * s + 6], axis=1))
        tans.append(jnp.concatenate(tan_parts[3 * s : 3 * s + 6], axis=1))
    square = sum(jnp.sum(m * m, axis=1, keepdims=True) for m in mains)
    cross = sum(jnp.sum(m * t, axis=1, keepdims=True) for m, t in zip(mains, tans))
    mean_square = square / total_width
    mean_cross = cross / total_width
    inv_rms = lax.rsqrt(mean_square + 1e-05)
    pull = inv_rms * inv_rms * inv_rms * mean_cross
    for i, (m, t) in enumerate(zip(mains, tans)):
        at = slice(i * 2 * width, (i + 1) * 2 * width)
        g = gain[:, at]
        normed[:, at] = (g * m * inv_rms).astype(BF16)
        normed_tan[:, at] = (g * (t * inv_rms - m * pull)).astype(BF16)


def whole(shape):
    return pl.BlockSpec(shape, lambda *_: (0,) * len(shape))


SMEM_SPEC = pl.BlockSpec(memory_space=pltpu.SMEM)


def local(xs, dxs, zgate, bmat, cmat, dt_raw, dt_bias, a_rate, d_skip, gain, traj_ids):
    tokens, inner = xs.shape
    heads = dt_raw.shape[0]
    blocks = tokens // Q
    wide = heads * LANES
    state_rows = bmat.shape[1]
    sources = lax.axis_size("head")
    seq_size = lax.axis_size("seq")
    group = state_rows // PACK
    groups = [list(range(g, g + group)) for g in range(0, seq_size, group)]
    params = pltpu.CompilerParams(vmem_limit_bytes=VMEM_BYTES)

    rows, cols, local_in, fin, send = pl.pallas_call(
        functools.partial(state_kernel, heads, blocks),
        out_shape=(
            jax.ShapeDtypeStruct((blocks * PACK, Q), F32),
            jax.ShapeDtypeStruct((tokens, LANES), F32),
            jax.ShapeDtypeStruct((blocks, state_rows, wide), BF16),
            jax.ShapeDtypeStruct((PACK, wide), F32),
            jax.ShapeDtypeStruct((state_rows, wide + LANES), BF16),
        ),
        in_specs=[SMEM_SPEC] * 3 + [pl.BlockSpec(memory_space=pltpu.VMEM)] * 4,
        compiler_params=params,
        cost_estimate=pl.CostEstimate(
            flops=300_000_000, bytes_accessed=4_000_000, transcendentals=30_000
        ),
    )(dt_bias, a_rate, traj_ids, xs, dxs, bmat, dt_raw)

    got = lax.all_to_all(
        send, "seq", split_axis=0, concat_axis=0, tiled=True, axis_index_groups=groups
    )
    back = pl.pallas_call(
        functools.partial(scan_kernel, heads, group),
        out_shape=jax.ShapeDtypeStruct((state_rows, wide), BF16),
        scratch_shapes=[pltpu.VMEM((state_rows, wide), F32)],
        compiler_params=params,
    )(got)
    incoming = lax.all_to_all(
        back, "seq", split_axis=0, concat_axis=0, tiled=True, axis_index_groups=groups
    )

    def token_block(width):
        return pl.BlockSpec((Q, width), lambda c: (c, 0))

    y_local = pl.pallas_call(
        functools.partial(diagonal_kernel, heads),
        grid=(blocks,),
        out_shape=jax.ShapeDtypeStruct((tokens, wide), F32),
        in_specs=[
            SMEM_SPEC,
            token_block(inner),
            token_block(inner),
            token_block(state_rows),
            token_block(state_rows),
            pl.BlockSpec((PACK, Q), lambda c: (c, 0)),
            token_block(LANES),
            pl.BlockSpec((1, state_rows, wide), lambda c: (c, 0, 0)),
        ],
        out_specs=token_block(wide),
        compiler_params=params,
        cost_estimate=pl.CostEstimate(
            flops=1_500_000_000, bytes_accessed=8_000_000, transcendentals=2_000_000
        ),
    )(d_skip, xs, dxs, bmat, cmat, rows, cols, local_in)

    gated = pl.pallas_call(
        functools.partial(gate_kernel, heads),
        grid=(blocks,),
        out_shape=jax.ShapeDtypeStruct((tokens, wide), BF16),
        in_specs=[
            token_block(wide),
            token_block(inner),
            token_block(state_rows),
            token_block(LANES),
            whole((PACK, wide)),
            whole((state_rows, wide)),
        ],
        out_specs=token_block(wide),
        compiler_params=params,
        cost_estimate=pl.CostEstimate(
            flops=260_000_000, bytes_accessed=8_000_000, transcendentals=500_000
        ),
    )(y_local, zgate, cmat, cols, fin, incoming)

    gathered = lax.all_to_all(gated, "head", split_axis=0, concat_axis=0, tiled=True)
    mine = tokens // sources
    strip = 16
    total = inner * sources
    return pl.pallas_call(
        functools.partial(norm_kernel, heads, sources, float(total)),
        grid=(mine // strip,),
        out_shape=(
            jax.ShapeDtypeStruct((mine, total), BF16),
            jax.ShapeDtypeStruct((mine, total), BF16),
        ),
        in_specs=[
            pl.BlockSpec((sources, strip, wide), lambda i: (0, i, 0)),
            whole((1, total)),
        ],
        out_specs=(
            pl.BlockSpec((strip, total), lambda i: (i, 0)),
            pl.BlockSpec((strip, total), lambda i: (i, 0)),
        ),
        compiler_params=params,
    )(gathered.reshape(sources, mine, wide), gain.reshape(1, total))


def solution(mesh):
    placed = (
        P("seq", "head"),
        P("seq", "head"),
        P("seq", "head"),
        P("seq", None),
        P("seq", None),
        P("head", "seq"),
        P("head"),
        P("head"),
        P("head"),
        P(),
        P("seq"),
    )
    return jax.shard_map(
        local,
        mesh=mesh,
        in_specs=placed,
        out_specs=(P(("seq", "head"), None), P(("seq", "head"), None)),
        check_vma=False,
    )
```

```python
import functools

import jax
import jax.numpy as jnp
from jax import lax
from jax.experimental import pallas as pl
from jax.experimental.pallas import tpu as pltpu
from jax.sharding import PartitionSpec as P

Q = 256
HALF = 128
LANES = 128
PACK = 8
LOG2E = 1.4426950408889634
MIB = 1024 * 1024
F32 = jnp.float32
BF16 = jnp.bfloat16


def column_of(values):
    place = lax.broadcasted_iota(jnp.int32, (PACK, 1), 0)
    column = jnp.zeros((PACK, 1), F32)
    for h, value in enumerate(values):
        column = jnp.where(place == h, value, column)
    return column


def by_head(per_head, rows):
    low = lax.broadcasted_iota(jnp.int32, (rows, LANES), 1) < LANES // 2
    first = jnp.where(low, per_head[0], per_head[1])
    second = jnp.where(low, per_head[2], per_head[3])
    last = jnp.broadcast_to(per_head[4], (rows, LANES))
    return [first, first, second, second, last]


def feature_rows(main, tan, heads, width):
    order = []
    for pair in range(0, heads, 2):
        for array in (main, tan):
            for h in range(pair, min(pair + 2, heads)):
                order.append((h, array[h * width : (h + 1) * width, :]))
    return order


def split_bf16(x, parts):
    pieces = []
    for _ in range(parts):
        piece = x.astype(BF16)
        pieces.append(piece)
        x = x - piece.astype(F32)
    return pieces


def across(left, right):
    return lax.dot_general(left, right, (((1,), (1,)), ((), ())), preferred_element_type=F32)


def state_kernel(
    heads,
    blocks,
    dt_bias,
    a_rate,
    traj,
    dt_raw,
    xs_hbm,
    dxs_hbm,
    bmat_hbm,
    shifted_out,
    logs_out,
    local_out,
    fin,
    send,
    xs,
    dxs,
    bmat,
    local_in,
    sems,
    out_sems,
):
    copies = [
        pltpu.make_async_copy(source, target, sems.at[i])
        for i, (source, target) in enumerate(
            ((xs_hbm, xs), (dxs_hbm, dxs), (bmat_hbm, bmat))
        )
    ]
    for copy in copies:
        copy.start()
    width = xs.shape[0] // heads
    bias = column_of([dt_bias[h] for h in range(heads)])
    rate = column_of([a_rate[h] * LOG2E for h in range(heads)])
    raw = jnp.concatenate([dt_raw[...], jnp.zeros((PACK - heads, blocks * Q), F32)], axis=0)
    pre = jnp.concatenate([raw[:, c * Q : (c + 1) * Q] for c in range(blocks)], axis=0)
    pre = pre + jnp.concatenate([bias] * blocks, axis=0)
    step = jnp.maximum(pre, 0.0) + jnp.log1p(jnp.exp(-jnp.abs(pre)))
    upper = (
        lax.broadcasted_iota(jnp.int32, (Q, Q), 0) <= lax.broadcasted_iota(jnp.int32, (Q, Q), 1)
    ).astype(BF16)
    logs = jnp.zeros((blocks * PACK, Q), F32)
    for piece in split_bf16(-(step * jnp.concatenate([rate] * blocks, axis=0)), 3)[::-1]:
        logs = logs + jnp.dot(piece, upper, preferred_element_type=F32)
    shifted = logs - jnp.log2(step)
    shifted_out[...] = shifted
    logs_out[...] = logs
    ends = logs[:, Q - 1 : Q]
    weight_in = jnp.exp2(ends - shifted)
    end_decay = jnp.exp2(ends)

    for copy in copies:
        copy.wait()
    state = jnp.zeros((LANES, heads * LANES), F32)
    factor = jnp.ones((PACK, 1), F32)
    copies_out = []
    for c in range(blocks):
        here = slice(c * Q, (c + 1) * Q)
        if c > 0:
            keep = jnp.where(traj[c] == traj[c - 1], 1.0, 0.0)
            state = state * keep
            factor = factor * keep
        local_in[c] = state.astype(BF16)
        leaving = pltpu.make_async_copy(local_in.at[c], local_out.at[c], out_sems.at[c])
        leaving.start()
        copies_out.append(leaving)
        fin[c * PACK : (c + 1) * PACK, :] = jnp.broadcast_to(factor, (PACK, LANES))
        weighted = jnp.concatenate(
            [
                (part.astype(F32) * weight_in[c * PACK + h : c * PACK + h + 1, :]).astype(BF16)
                for h, part in feature_rows(xs[:, here], dxs[:, here], heads, width)
            ],
            axis=0,
        )
        gained = across(bmat[here, :].T, weighted)
        ended = end_decay[c * PACK : (c + 1) * PACK, :]
        decay = by_head([ended[h : h + 1, :] for h in range(heads)], 1)
        state = state * jnp.concatenate(decay, axis=1) + gained
        factor = factor * ended
    lane = lax.broadcasted_iota(jnp.int32, (1, LANES), 1)
    notes = jnp.zeros((1, LANES), F32)
    for h in range(heads):
        rest = factor[h : h + 1, :]
        for k in range(3):
            piece = rest.astype(BF16).astype(F32)
            notes = jnp.where(lane == k * heads + h, piece, notes)
            rest = rest - piece
    notes = jnp.where(lane == 3 * heads, traj[0].astype(F32), notes)
    notes = jnp.where(lane == 3 * heads + 1, traj[blocks - 1].astype(F32), notes)
    send[:, : heads * LANES] = state.astype(BF16)
    send[:, heads * LANES :] = jnp.broadcast_to(notes, (LANES, LANES)).astype(BF16)
    for leaving in copies_out:
        leaving.wait()


def scan_kernel(heads, count, got, _, back, hold):
    width = heads * LANES
    everything = got[...].astype(F32)
    carried = jnp.zeros((PACK, width), F32)
    last_id = None
    for s in range(count):
        at = slice(s * PACK, (s + 1) * PACK)
        notes = everything[at, width:]
        factor = []
        for h in range(heads):
            total = notes[:, h : h + 1]
            for k in range(1, 3):
                total = total + notes[:, k * heads + h : k * heads + h + 1]
            factor.append(total)
        first_id = notes[:, 3 * heads : 3 * heads + 1]
        if s > 0:
            carried = jnp.where(first_id == last_id, carried, 0.0)
        hold[at, :] = carried
        last_id = notes[:, 3 * heads + 1 : 3 * heads + 2]
        carried = jnp.concatenate(by_head(factor, PACK), axis=1) * carried + everything[at, :width]
    back[...] = hold[...].astype(BF16)


def diagonal_kernel(
    heads, d_skip, xs, dxs, bmat, cmat, shifted, logs, local_in, fin, y_local, reach, token
):
    width = xs.shape[0] // heads
    decays = jnp.exp2(logs[...])
    table = jnp.concatenate(
        [logs[...], decays, decays * fin[:, 0:1], jnp.zeros((LANES - 3 * PACK, Q), F32)], axis=0
    ).T
    reach[...] = table
    token[...] = table[:PACK, :]
    scores = across(cmat[...], bmat[...])
    causal = lax.broadcasted_iota(jnp.int32, (HALF, HALF), 0) >= lax.broadcasted_iota(
        jnp.int32, (HALF, HALF), 1
    )
    unit = (
        lax.broadcasted_iota(jnp.int32, (Q, Q), 0) == lax.broadcasted_iota(jnp.int32, (Q, Q), 1)
    ).astype(BF16)
    joined = jnp.concatenate(
        [part for _, part in feature_rows(xs[...], dxs[...], heads, width)], axis=0
    )
    plain = across(unit, joined)
    low = lax.broadcasted_iota(jnp.int32, (Q, LANES), 1) < LANES // 2
    sums = []
    for h in range(heads):
        log_t = table[:, h : h + 1]
        log_s = shifted[h : h + 1, :]
        near = jnp.where(
            causal, scores[:HALF, :HALF] * jnp.exp2(log_t[:HALF] - log_s[:, :HALF]), 0.0
        )
        far = scores[HALF:, :HALF] * jnp.exp2(log_t[HALF:] - log_s[:, :HALF])
        last = jnp.where(
            causal, scores[HALF:, HALF:] * jnp.exp2(log_t[HALF:] - log_s[:, HALF:]), 0.0
        )
        operand = joined[(h // 2) * 2 * LANES : (h // 2 + 1) * 2 * LANES]
        top = across(near.astype(BF16), operand[:, :HALF])
        bottom = across(jnp.concatenate([far, last], axis=1).astype(BF16), operand)
        sums.append(jnp.concatenate([top, bottom], axis=0))
    diagonal = []
    for pair in range(heads // 2):
        left, right = sums[2 * pair], sums[2 * pair + 1]
        diagonal.append(jnp.where(low, left[:, :LANES], right[:, :LANES]))
        diagonal.append(jnp.where(low, left[:, LANES:], right[:, LANES:]))
    diagonal.append(sums[heads - 1])
    carried = jnp.dot(cmat[...], local_in[0], preferred_element_type=F32)
    decay = by_head([table[:, PACK + h : PACK + h + 1] for h in range(heads)], Q)
    skip = by_head([d_skip[h] for h in range(heads)], 1)
    for i in range(heads):
        at = slice(i * LANES, (i + 1) * LANES)
        y_local[:, at] = diagonal[i] + carried[:, at] * decay[i] + plain[:, at] * skip[i]


def prepare_kernel(heads, zgate, y_local, reach, _, base, slope):
    unit = (
        lax.broadcasted_iota(jnp.int32, (Q, Q), 0) == lax.broadcasted_iota(jnp.int32, (Q, Q), 1)
    ).astype(BF16)
    z = across(unit, zgate[...])
    gate = z / (1.0 + jnp.exp(-z))
    gate_last = gate[:, 2 * LANES :]
    gates = [gate[:, :LANES], gate[:, LANES : 2 * LANES]]
    gates = [gates[0], gates[0], gates[1], gates[1]]
    gates.append(jnp.concatenate([gate_last, gate_last], axis=1))
    reached = by_head([reach[:, 2 * PACK + h : 2 * PACK + h + 1] for h in range(heads)], Q)
    for i in range(heads):
        at = slice(i * LANES, (i + 1) * LANES)
        base[:, at] = y_local[:, at] * gates[i]
        slope[:, at] = (reached[i] * gates[i]).astype(BF16)


def gate_kernel(base, slope, cmat, incoming, out):
    carried = jnp.dot(cmat[...], incoming[...], preferred_element_type=F32)
    out[...] = (base[...] + carried * slope[...].astype(F32)).astype(BF16)


def norm_kernel(heads, sources, total_width, gathered, gain, normed, normed_tan):
    main_parts, tan_parts = [], []
    half = LANES // 2
    for s in range(sources):
        tiles = [
            gathered[s, :, i * LANES : (i + 1) * LANES].astype(F32) for i in range(heads)
        ]
        main_parts += [tiles[0], tiles[2], tiles[4][:, :half]]
        tan_parts += [tiles[1], tiles[3], tiles[4][:, half:]]
    width = heads * half
    mains, tans = [], []
    for s in range(0, sources, 2):
        mains.append(jnp.concatenate(main_parts[3 * s : 3 * s + 6], axis=1))
        tans.append(jnp.concatenate(tan_parts[3 * s : 3 * s + 6], axis=1))
    square = sum(jnp.sum(m * m, axis=1, keepdims=True) for m in mains)
    cross = sum(jnp.sum(m * t, axis=1, keepdims=True) for m, t in zip(mains, tans))
    mean_square = square / total_width
    mean_cross = cross / total_width
    inv_rms = lax.rsqrt(mean_square + 1e-05)
    pull = inv_rms * inv_rms * inv_rms * mean_cross
    for i, (m, t) in enumerate(zip(mains, tans)):
        at = slice(i * 2 * width, (i + 1) * 2 * width)
        g = gain[:, at]
        normed[:, at] = (g * m * inv_rms).astype(BF16)
        normed_tan[:, at] = (g * (t * inv_rms - m * pull)).astype(BF16)


def whole(shape):
    return pl.BlockSpec(shape, lambda *_: (0,) * len(shape))


SMEM_SPEC = pl.BlockSpec(memory_space=pltpu.SMEM)


def local(xs, dxs, zgate, bmat, cmat, dt_raw, dt_bias, a_rate, d_skip, gain, traj_ids):
    tokens, inner = xs.shape
    heads = dt_raw.shape[0]
    blocks = tokens // Q
    wide = heads * LANES
    state_rows = bmat.shape[1]
    sources = lax.axis_size("head")
    seq_size = lax.axis_size("seq")
    group = state_rows // PACK
    groups = [list(range(g, g + group)) for g in range(0, seq_size, group)]
    params = pltpu.CompilerParams(vmem_limit_bytes=60 * MIB)
    small = pltpu.CompilerParams(vmem_limit_bytes=16 * MIB)
    roomy = pltpu.CompilerParams(vmem_limit_bytes=56 * MIB)
    in_vmem = pl.BlockSpec(memory_space=pltpu.VMEM)
    in_hbm = pl.BlockSpec(memory_space=pl.ANY)
    xs, dxs, zgate = xs.T, dxs.T, zgate.T

    shifted, logs, local_in, fin, send = pl.pallas_call(
        functools.partial(state_kernel, heads, blocks),
        out_shape=(
            jax.ShapeDtypeStruct((blocks * PACK, Q), F32),
            jax.ShapeDtypeStruct((blocks * PACK, Q), F32),
            jax.ShapeDtypeStruct((blocks, state_rows, wide), BF16),
            jax.ShapeDtypeStruct((blocks * PACK, LANES), F32),
            jax.ShapeDtypeStruct((state_rows, wide + LANES), BF16),
        ),
        in_specs=[SMEM_SPEC] * 3 + [in_vmem] + [in_hbm] * 3,
        out_specs=(in_vmem, in_vmem, in_hbm, in_vmem, in_vmem),
        scratch_shapes=[
            pltpu.VMEM((inner, tokens), BF16),
            pltpu.VMEM((inner, tokens), BF16),
            pltpu.VMEM((tokens, state_rows), BF16),
            pltpu.VMEM((blocks, state_rows, wide), BF16),
            pltpu.SemaphoreType.DMA((3,)),
            pltpu.SemaphoreType.DMA((blocks,)),
        ],
        compiler_params=params,
        cost_estimate=pl.CostEstimate(
            flops=300_000_000, bytes_accessed=4_000_000, transcendentals=30_000
        ),
    )(dt_bias, a_rate, traj_ids, dt_raw, xs, dxs, bmat)

    def token_block(width):
        return pl.BlockSpec((Q, width), lambda c: (c, 0))

    def feature_block(width):
        return pl.BlockSpec((width, Q), lambda c: (0, c))

    y_local, reach, token = pl.pallas_call(
        functools.partial(diagonal_kernel, heads),
        grid=(blocks,),
        out_shape=(
            jax.ShapeDtypeStruct((tokens, wide), F32),
            jax.ShapeDtypeStruct((tokens, LANES), F32),
            jax.ShapeDtypeStruct((PACK, LANES), F32),
        ),
        in_specs=[
            SMEM_SPEC,
            feature_block(inner),
            feature_block(inner),
            token_block(state_rows),
            token_block(state_rows),
            pl.BlockSpec((PACK, Q), lambda c: (c, 0)),
            pl.BlockSpec((PACK, Q), lambda c: (c, 0)),
            pl.BlockSpec((1, state_rows, wide), lambda c: (c, 0, 0)),
            pl.BlockSpec((PACK, LANES), lambda c: (c, 0)),
        ],
        out_specs=(token_block(wide), token_block(LANES), whole((PACK, LANES))),
        compiler_params=params,
        cost_estimate=pl.CostEstimate(
            flops=2_000_000_000, bytes_accessed=16_000_000, transcendentals=2_000_000
        ),
    )(d_skip, xs, dxs, bmat, cmat, shifted, logs, local_in, fin)

    got = lax.all_to_all(
        send, "seq", split_axis=0, concat_axis=0, tiled=True, axis_index_groups=groups
    )
    back = pl.pallas_call(
        functools.partial(scan_kernel, heads, group),
        out_shape=jax.ShapeDtypeStruct((state_rows, wide), BF16),
        in_specs=[in_vmem, in_hbm],
        scratch_shapes=[pltpu.VMEM((state_rows, wide), F32)],
        compiler_params=small,
    )(got, token)
    incoming = lax.all_to_all(
        back, "seq", split_axis=0, concat_axis=0, tiled=True, axis_index_groups=groups
    )
    base, slope = pl.pallas_call(
        functools.partial(prepare_kernel, heads),
        grid=(blocks,),
        out_shape=(
            jax.ShapeDtypeStruct((tokens, wide), F32),
            jax.ShapeDtypeStruct((tokens, wide), BF16),
        ),
        in_specs=[
            feature_block(inner),
            token_block(wide),
            token_block(LANES),
            in_hbm,
        ],
        out_specs=(token_block(wide), token_block(wide)),
        compiler_params=params,
        cost_estimate=pl.CostEstimate(
            flops=300_000_000, bytes_accessed=16_000_000, transcendentals=500_000
        ),
    )(zgate, y_local, reach, back)

    gated = pl.pallas_call(
        gate_kernel,
        grid=(blocks,),
        out_shape=jax.ShapeDtypeStruct((tokens, wide), BF16),
        in_specs=[
            token_block(wide),
            token_block(wide),
            token_block(state_rows),
            whole((state_rows, wide)),
        ],
        out_specs=token_block(wide),
        compiler_params=roomy,
        cost_estimate=pl.CostEstimate(
            flops=260_000_000, bytes_accessed=8_000_000, transcendentals=0
        ),
    )(base, slope, cmat, incoming)

    gathered = lax.all_to_all(gated, "head", split_axis=0, concat_axis=0, tiled=True)
    mine = tokens // sources
    strip = 16
    total = inner * sources
    return pl.pallas_call(
        functools.partial(norm_kernel, heads, sources, float(total)),
        grid=(mine // strip,),
        out_shape=(
            jax.ShapeDtypeStruct((mine, total), BF16),
            jax.ShapeDtypeStruct((mine, total), BF16),
        ),
        in_specs=[
            pl.BlockSpec((sources, strip, wide), lambda i: (0, i, 0)),
            whole((1, total)),
        ],
        out_specs=(
            pl.BlockSpec((strip, total), lambda i: (i, 0)),
            pl.BlockSpec((strip, total), lambda i: (i, 0)),
        ),
        compiler_params=params,
    )(gathered.reshape(sources, mine, wide), gain.reshape(1, total))


def solution(mesh):
    placed = (
        P("seq", "head"),
        P("seq", "head"),
        P("seq", "head"),
        P("seq", None),
        P("seq", None),
        P("head", "seq"),
        P("head"),
        P("head"),
        P("head"),
        P(),
        P("seq"),
    )
    return jax.shard_map(
        local,
        mesh=mesh,
        in_specs=placed,
        out_specs=(P(("seq", "head"), None), P(("seq", "head"), None)),
        check_vma=False,
    )
```

```python
import functools

import jax
import jax.numpy as jnp
from jax import lax
from jax.experimental import pallas as pl
from jax.experimental.pallas import tpu as pltpu
from jax.sharding import PartitionSpec as P

Q = 256
HALF = 128
LANES = 128
PACK = 8
LOG2E = 1.4426950408889634
MIB = 1024 * 1024
F32 = jnp.float32
BF16 = jnp.bfloat16


def column_of(values):
    place = lax.broadcasted_iota(jnp.int32, (PACK, 1), 0)
    column = jnp.zeros((PACK, 1), F32)
    for h, value in enumerate(values):
        column = jnp.where(place == h, value, column)
    return column


def by_head(per_head, rows):
    low = lax.broadcasted_iota(jnp.int32, (rows, LANES), 1) < LANES // 2
    first = jnp.where(low, per_head[0], per_head[1])
    second = jnp.where(low, per_head[2], per_head[3])
    last = jnp.broadcast_to(per_head[4], (rows, LANES))
    return [first, first, second, second, last]


def feature_rows(main, tan, heads, width):
    order = []
    for pair in range(0, heads, 2):
        for array in (main, tan):
            for h in range(pair, min(pair + 2, heads)):
                order.append((h, array[h * width : (h + 1) * width, :]))
    return order


def split_bf16(x, parts):
    pieces = []
    for _ in range(parts):
        piece = x.astype(BF16)
        pieces.append(piece)
        x = x - piece.astype(F32)
    return pieces


def across(left, right):
    return lax.dot_general(left, right, (((1,), (1,)), ((), ())), preferred_element_type=F32)


def state_kernel(
    heads,
    blocks,
    dt_bias,
    a_rate,
    traj,
    dt_raw,
    xs_hbm,
    dxs_hbm,
    bmat_hbm,
    shifted_out,
    logs_out,
    local_out,
    fin,
    send,
    xs,
    dxs,
    bmat,
    local_in,
    sems,
    out_sems,
):
    width = xs.shape[0] // heads
    chunks = [slice(h * width, min(h + 2, heads) * width) for h in range(0, heads, 2)]
    b_copy = pltpu.make_async_copy(bmat_hbm, bmat, sems.at[2, 0])
    copies = []
    for i, at in enumerate(chunks):
        copies.append(
            [
                pltpu.make_async_copy(xs_hbm.at[at, :], xs.at[at, :], sems.at[0, i]),
                pltpu.make_async_copy(dxs_hbm.at[at, :], dxs.at[at, :], sems.at[1, i]),
            ]
        )
    copies[0][0].start()
    copies[0][1].start()
    b_copy.start()
    for pair_copies in copies[1:]:
        for copy in pair_copies:
            copy.start()
    bias = column_of([dt_bias[h] for h in range(heads)])
    rate = column_of([a_rate[h] * LOG2E for h in range(heads)])
    raw = jnp.concatenate([dt_raw[...], jnp.zeros((PACK - heads, blocks * Q), F32)], axis=0)
    pre = jnp.concatenate([raw[:, c * Q : (c + 1) * Q] for c in range(blocks)], axis=0)
    pre = pre + jnp.concatenate([bias] * blocks, axis=0)
    step = jnp.maximum(pre, 0.0) + jnp.log1p(jnp.exp(-jnp.abs(pre)))
    upper = (
        lax.broadcasted_iota(jnp.int32, (Q, Q), 0) <= lax.broadcasted_iota(jnp.int32, (Q, Q), 1)
    ).astype(BF16)
    logs = jnp.zeros((blocks * PACK, Q), F32)
    for piece in split_bf16(-(step * jnp.concatenate([rate] * blocks, axis=0)), 3)[::-1]:
        logs = logs + jnp.dot(piece, upper, preferred_element_type=F32)
    shifted = logs - jnp.log2(step)
    shifted_out[...] = shifted
    logs_out[...] = logs
    ends = logs[:, Q - 1 : Q]
    weight_in = jnp.exp2(ends - shifted)
    end_decay = jnp.exp2(ends)

    factor = jnp.ones((PACK, 1), F32)
    keeps = [None]
    for c in range(blocks):
        if c > 0:
            keeps.append(jnp.where(traj[c] == traj[c - 1], 1.0, 0.0))
            factor = factor * keeps[c]
        fin[c * PACK : (c + 1) * PACK, :] = jnp.broadcast_to(factor, (PACK, LANES))
        factor = factor * end_decay[c * PACK : (c + 1) * PACK, :]
    copies_out = []
    b_copy.wait()
    for i, at in enumerate(chunks):
        for copy in copies[i]:
            copy.wait()
        members = [h for h in range(2 * i, min(2 * i + 2, heads))] * 2
        place = slice(2 * at.start, 2 * at.stop)
        state = jnp.zeros((len(members) * width, LANES), F32)
        for c in range(blocks):
            here = slice(c * Q, (c + 1) * Q)
            if c > 0:
                state = state * keeps[c]
            local_in[c, place, :] = state.astype(BF16)
            both = jnp.concatenate([xs[at, here], dxs[at, here]], axis=0).astype(F32)
            scale = jnp.concatenate(
                [
                    jnp.broadcast_to(
                        weight_in[c * PACK + h : c * PACK + h + 1, :], (width, Q)
                    )
                    for h in members
                ],
                axis=0,
            )
            gained = jnp.dot(
                (both * scale).astype(BF16), bmat[here, :], preferred_element_type=F32
            )
            decay = jnp.concatenate(
                [
                    jnp.broadcast_to(
                        end_decay[c * PACK + h : c * PACK + h + 1, :], (width, LANES)
                    )
                    for h in members
                ],
                axis=0,
            )
            state = state * decay + gained
        rows = pl.ds(place.start, place.stop - place.start)
        leaving = pltpu.make_async_copy(
            local_in.at[:, rows, :], local_out.at[:, rows, :], out_sems.at[i]
        )
        leaving.start()
        copies_out.append(leaving)
        send[:, place] = state.T.astype(BF16)
    lane = lax.broadcasted_iota(jnp.int32, (1, LANES), 1)
    notes = jnp.zeros((1, LANES), F32)
    for h in range(heads):
        rest = factor[h : h + 1, :]
        for k in range(3):
            piece = rest.astype(BF16).astype(F32)
            notes = jnp.where(lane == k * heads + h, piece, notes)
            rest = rest - piece
    notes = jnp.where(lane == 3 * heads, traj[0].astype(F32), notes)
    notes = jnp.where(lane == 3 * heads + 1, traj[blocks - 1].astype(F32), notes)
    send[:, heads * LANES :] = jnp.broadcast_to(notes, (LANES, LANES)).astype(BF16)
    for leaving in copies_out:
        leaving.wait()


def scan_kernel(heads, count, got, _, back, hold):
    width = heads * LANES
    everything = got[...].astype(F32)
    carried = jnp.zeros((PACK, width), F32)
    last_id = None
    for s in range(count):
        at = slice(s * PACK, (s + 1) * PACK)
        notes = everything[at, width:]
        factor = []
        for h in range(heads):
            total = notes[:, h : h + 1]
            for k in range(1, 3):
                total = total + notes[:, k * heads + h : k * heads + h + 1]
            factor.append(total)
        first_id = notes[:, 3 * heads : 3 * heads + 1]
        if s > 0:
            carried = jnp.where(first_id == last_id, carried, 0.0)
        hold[at, :] = carried
        last_id = notes[:, 3 * heads + 1 : 3 * heads + 2]
        carried = jnp.concatenate(by_head(factor, PACK), axis=1) * carried + everything[at, :width]
    back[...] = hold[...].astype(BF16)


def diagonal_kernel(
    heads, d_skip, xs, dxs, zgate, bmat, cmat, shifted, logs, local_in, fin, base, slope
):
    width = xs.shape[0] // heads
    block = pl.program_id(0)
    mine = pl.ds(pl.multiple_of(block * PACK, PACK), PACK)
    log_rows, shifted_rows = logs[mine, :], shifted[mine, :]
    decays = jnp.exp2(log_rows)
    table = jnp.concatenate(
        [log_rows, decays, decays * fin[mine, 0:1], jnp.zeros((LANES - 3 * PACK, Q), F32)], axis=0
    ).T
    scores = across(cmat[...], bmat[...])
    causal = lax.broadcasted_iota(jnp.int32, (HALF, HALF), 0) >= lax.broadcasted_iota(
        jnp.int32, (HALF, HALF), 1
    )
    unit = (
        lax.broadcasted_iota(jnp.int32, (Q, Q), 0) == lax.broadcasted_iota(jnp.int32, (Q, Q), 1)
    ).astype(BF16)
    nothing = jnp.zeros((HALF, HALF), BF16)
    z = across(unit, zgate[...])
    gate = z / (1.0 + jnp.exp(-z))
    gate_last = gate[:, 2 * LANES :]
    gates = [
        gate[:, :LANES],
        gate[:, LANES : 2 * LANES],
        jnp.concatenate([gate_last, gate_last], axis=1),
    ]
    low = lax.broadcasted_iota(jnp.int32, (Q, LANES), 1) < LANES // 2

    def weights(h):
        log_t = table[:, h : h + 1]
        log_s = shifted_rows[h : h + 1, :]
        near = scores[:HALF, :HALF] * jnp.exp2(log_t[:HALF] - log_s[:, :HALF])
        far = scores[HALF:, :HALF] * jnp.exp2(log_t[HALF:] - log_s[:, :HALF])
        last = scores[HALF:, HALF:] * jnp.exp2(log_t[HALF:] - log_s[:, HALF:])
        top = jnp.concatenate([jnp.where(causal, near, 0.0).astype(BF16), nothing], axis=1)
        bottom = jnp.concatenate([far, jnp.where(causal, last, 0.0)], axis=1).astype(BF16)
        return [top, bottom]

    carried = across(cmat[...], local_in[0])
    decay = by_head([table[:, PACK + h : PACK + h + 1] for h in range(heads)], Q)
    reach = by_head([table[:, 2 * PACK + h : 2 * PACK + h + 1] for h in range(heads)], Q)
    skip = by_head([d_skip[h] for h in range(heads)], 1)
    rows = feature_rows(xs[...], dxs[...], heads, width)
    for pair in range(0, heads, 2):
        members = range(pair, min(pair + 2, heads))
        operand = jnp.concatenate([part for h, part in rows if h in members], axis=0)
        left = [piece for h in members for piece in weights(h)] + [unit]
        sums = across(jnp.concatenate(left, axis=0), operand)
        count = len(members)
        for i in range(count):
            tile = pair + i
            at = slice(tile * LANES, (tile + 1) * LANES)
            lanes = slice(i * LANES, (i + 1) * LANES)
            diagonal = sums[:Q, lanes]
            if count == 2:
                diagonal = jnp.where(low, diagonal, sums[Q : 2 * Q, lanes])
            plain = sums[count * Q :, lanes]
            y = diagonal + carried[:, at] * decay[tile] + plain * skip[tile]
            base[:, at] = (y * gates[pair // 2]).astype(BF16)
        at = slice(pair // 2 * LANES, (pair // 2 + 1) * LANES)
        slope[:, at] = (reach[pair] * gates[pair // 2]).astype(BF16)


def gate_kernel(blocks, heads, base, slope, cmat_hbm, incoming, out, cmat, sems):
    copies = []
    for c in range(blocks):
        here = pl.ds(c * Q, Q)
        copies.append(
            pltpu.make_async_copy(cmat_hbm.at[here, :], cmat.at[here, :], sems.at[c])
        )
    for copy in copies:
        copy.start()
    state = incoming[...]
    for c in range(blocks):
        here = slice(c * Q, (c + 1) * Q)
        copies[c].wait()
        carried = jnp.dot(cmat[here, :], state, preferred_element_type=F32)
        for i in range(heads):
            at = slice(i * LANES, (i + 1) * LANES)
            gain = slope[here, i // 2 * LANES : (i // 2 + 1) * LANES].astype(F32)
            out[here, at] = (base[here, at].astype(F32) + carried[:, at] * gain).astype(BF16)


def norm_kernel(
    heads, sources, strip, strips, total_width, gathered, gain, normed, normed_tan, held, sems
):
    half = LANES // 2
    width = heads * half
    copies = []
    for r in range(strips):
        here = slice(r * strip, (r + 1) * strip)
        main_parts, tan_parts = [], []
        for s in range(sources):
            tiles = [
                gathered[s, here, i * LANES : (i + 1) * LANES].astype(F32) for i in range(heads)
            ]
            main_parts += [tiles[0], tiles[2], tiles[4][:, :half]]
            tan_parts += [tiles[1], tiles[3], tiles[4][:, half:]]
        mains, tans = [], []
        for s in range(0, sources, 2):
            mains.append(jnp.concatenate(main_parts[3 * s : 3 * s + 6], axis=1))
            tans.append(jnp.concatenate(tan_parts[3 * s : 3 * s + 6], axis=1))
        square = sum(m * m for m in mains)
        cross = sum(m * t for m, t in zip(mains, tans))
        mean_square = jnp.sum(square, axis=1, keepdims=True) / total_width
        mean_cross = jnp.sum(cross, axis=1, keepdims=True) / total_width
        inv_rms = lax.rsqrt(mean_square + 1e-05)
        pull = inv_rms * inv_rms * inv_rms * mean_cross
        for i, (m, t) in enumerate(zip(mains, tans)):
            at = slice(i * 2 * width, (i + 1) * 2 * width)
            g = gain[:, at]
            held[0, here, at] = (g * m * inv_rms).astype(BF16)
            held[1, here, at] = (g * (t * inv_rms - m * pull)).astype(BF16)
        for k, target in enumerate((normed, normed_tan)):
            copy = pltpu.make_async_copy(held.at[k, here, :], target.at[here, :], sems.at[k, r])
            copy.start()
            copies.append(copy)
    for copy in copies:
        copy.wait()


def whole(shape):
    return pl.BlockSpec(shape, lambda *_: (0,) * len(shape))


SMEM_SPEC = pl.BlockSpec(memory_space=pltpu.SMEM)


def local(xs, dxs, zgate, bmat, cmat, dt_raw, dt_bias, a_rate, d_skip, gain, traj_ids):
    tokens, inner = xs.shape
    heads = dt_raw.shape[0]
    blocks = tokens // Q
    wide = heads * LANES
    state_rows = bmat.shape[1]
    sources = lax.axis_size("head")
    seq_size = lax.axis_size("seq")
    group = state_rows // PACK
    groups = [list(range(g, g + group)) for g in range(0, seq_size, group)]
    params = pltpu.CompilerParams(vmem_limit_bytes=60 * MIB)
    roomy = pltpu.CompilerParams(vmem_limit_bytes=32 * MIB)
    small = pltpu.CompilerParams(vmem_limit_bytes=16 * MIB)
    in_vmem = pl.BlockSpec(memory_space=pltpu.VMEM)
    in_hbm = pl.BlockSpec(memory_space=pl.ANY)
    xs, dxs, zgate, bmat, cmat = [
        pltpu.with_memory_space_constraint(array, pltpu.HBM)
        for array in (xs.T, dxs.T, zgate.T, bmat, cmat)
    ]

    def pinned(array):
        return pltpu.with_memory_space_constraint(array, pltpu.VMEM)

    shifted, logs, local_in, fin, send = pl.pallas_call(
        functools.partial(state_kernel, heads, blocks),
        out_shape=(
            pltpu.VMEM((blocks * PACK, Q), F32),
            pltpu.VMEM((blocks * PACK, Q), F32),
            jax.ShapeDtypeStruct((blocks, wide, state_rows), BF16),
            pltpu.VMEM((blocks * PACK, LANES), F32),
            pltpu.VMEM((state_rows, wide + LANES), BF16),
        ),
        in_specs=[SMEM_SPEC] * 3 + [in_vmem] + [in_hbm] * 3,
        out_specs=(in_vmem, in_vmem, in_hbm, in_vmem, in_vmem),
        scratch_shapes=[
            pltpu.VMEM((inner, tokens), BF16),
            pltpu.VMEM((inner, tokens), BF16),
            pltpu.VMEM((tokens, state_rows), BF16),
            pltpu.VMEM((blocks, wide, state_rows), BF16),
            pltpu.SemaphoreType.DMA((3, len(range(0, heads, 2)))),
            pltpu.SemaphoreType.DMA((len(range(0, heads, 2)),)),
        ],
        compiler_params=params,
        cost_estimate=pl.CostEstimate(
            flops=300_000_000, bytes_accessed=4_000_000, transcendentals=30_000
        ),
    )(dt_bias, a_rate, traj_ids, dt_raw, xs, dxs, bmat)

    def token_block(width):
        return pl.BlockSpec((Q, width), lambda c: (c, 0))

    def feature_block(width):
        return pl.BlockSpec((width, Q), lambda c: (0, c))

    lean = (heads + 1) // 2 * LANES
    base, slope = pl.pallas_call(
        functools.partial(diagonal_kernel, heads),
        grid=(blocks,),
        out_shape=(
            pltpu.VMEM((tokens, wide), BF16),
            pltpu.VMEM((tokens, lean), BF16),
        ),
        in_specs=[
            SMEM_SPEC,
            feature_block(inner),
            feature_block(inner),
            feature_block(inner),
            token_block(state_rows),
            token_block(state_rows),
            in_vmem,
            in_vmem,
            pl.BlockSpec((1, wide, state_rows), lambda c: (c, 0, 0)),
            in_vmem,
        ],
        out_specs=(token_block(wide), token_block(lean)),
        compiler_params=roomy,
        cost_estimate=pl.CostEstimate(
            flops=2_000_000_000, bytes_accessed=16_000_000, transcendentals=2_000_000
        ),
    )(
        d_skip,
        xs,
        dxs,
        zgate,
        bmat,
        cmat,
        pinned(shifted),
        pinned(logs),
        pltpu.with_memory_space_constraint(local_in, pltpu.HBM),
        pinned(fin),
    )

    got = lax.all_to_all(
        send, "seq", split_axis=0, concat_axis=0, tiled=True, axis_index_groups=groups
    )
    back = pl.pallas_call(
        functools.partial(scan_kernel, heads, group),
        out_shape=jax.ShapeDtypeStruct((state_rows, wide), BF16),
        in_specs=[in_vmem, in_hbm],
        scratch_shapes=[pltpu.VMEM((state_rows, wide), F32)],
        compiler_params=small,
    )(got, pinned(slope))
    incoming = lax.all_to_all(
        back, "seq", split_axis=0, concat_axis=0, tiled=True, axis_index_groups=groups
    )
    gated = pl.pallas_call(
        functools.partial(gate_kernel, blocks, heads),
        out_shape=jax.ShapeDtypeStruct((tokens, wide), BF16),
        in_specs=[in_vmem, in_vmem, in_hbm, in_vmem],
        scratch_shapes=[
            pltpu.VMEM((tokens, state_rows), BF16),
            pltpu.SemaphoreType.DMA((blocks,)),
        ],
        compiler_params=small,
        cost_estimate=pl.CostEstimate(
            flops=260_000_000, bytes_accessed=6_000_000, transcendentals=0
        ),
    )(
        pinned(base),
        pinned(slope),
        cmat,
        incoming,
    )

    gathered = lax.all_to_all(gated, "head", split_axis=0, concat_axis=0, tiled=True)
    mine = tokens // sources
    strip = 16
    strips = mine // strip
    total = inner * sources
    return pl.pallas_call(
        functools.partial(norm_kernel, heads, sources, strip, strips, float(total)),
        out_shape=(
            jax.ShapeDtypeStruct((mine, total), BF16),
            jax.ShapeDtypeStruct((mine, total), BF16),
        ),
        in_specs=[in_vmem] * 2,
        out_specs=(in_hbm, in_hbm),
        scratch_shapes=[
            pltpu.VMEM((2, mine, total), BF16),
            pltpu.SemaphoreType.DMA((2, strips)),
        ],
        compiler_params=small,
    )(gathered.reshape(sources, mine, wide), gain.reshape(1, total))


def solution(mesh):
    placed = (
        P("seq", "head"),
        P("seq", "head"),
        P("seq", "head"),
        P("seq", None),
        P("seq", None),
        P("head", "seq"),
        P("head"),
        P("head"),
        P("head"),
        P(),
        P("seq"),
    )
    return jax.shard_map(
        local,
        mesh=mesh,
        in_specs=placed,
        out_specs=(P(("seq", "head"), None), P(("seq", "head"), None)),
        check_vma=False,
    )
```

```python
import functools

import jax
import jax.numpy as jnp
from jax import lax
from jax.experimental import pallas as pl
from jax.experimental.pallas import tpu as pltpu
from jax.sharding import PartitionSpec as P

Q = 256
HALF = 128
LANES = 128
PACK = 8
LOG2E = 1.4426950408889634
MIB = 1024 * 1024
F32 = jnp.float32
BF16 = jnp.bfloat16


def column_of(values):
    place = lax.broadcasted_iota(jnp.int32, (PACK, 1), 0)
    column = jnp.zeros((PACK, 1), F32)
    for h, value in enumerate(values):
        column = jnp.where(place == h, value, column)
    return column


def by_head(per_head, rows):
    low = lax.broadcasted_iota(jnp.int32, (rows, LANES), 1) < LANES // 2
    first = jnp.where(low, per_head[0], per_head[1])
    second = jnp.where(low, per_head[2], per_head[3])
    last = jnp.broadcast_to(per_head[4], (rows, LANES))
    return [first, first, second, second, last]


def feature_rows(main, tan, heads, width):
    order = []
    for pair in range(0, heads, 2):
        for array in (main, tan):
            for h in range(pair, min(pair + 2, heads)):
                order.append((h, array[h * width : (h + 1) * width, :]))
    return order


def split_bf16(x, parts):
    pieces = []
    for _ in range(parts):
        piece = x.astype(BF16)
        pieces.append(piece)
        x = x - piece.astype(F32)
    return pieces


def across(left, right):
    return lax.dot_general(left, right, (((1,), (1,)), ((), ())), preferred_element_type=F32)


def state_kernel(
    heads,
    blocks,
    dt_bias,
    a_rate,
    traj,
    dt_hbm,
    xs_hbm,
    dxs_hbm,
    bmat_hbm,
    shifted_out,
    logs_out,
    local_out,
    fin,
    send,
    xs,
    dxs,
    bmat,
    local_in,
    dt_raw,
    sems,
    out_sems,
):
    width = xs.shape[0] // heads
    chunks = [slice(h * width, min(h + 2, heads) * width) for h in range(0, heads, 2)]
    b_copy = pltpu.make_async_copy(bmat_hbm, bmat, sems.at[2, 0])
    dt_copy = pltpu.make_async_copy(dt_hbm, dt_raw, sems.at[2, 1])
    dt_copy.start()
    copies = []
    for i, at in enumerate(chunks):
        copies.append(
            [
                pltpu.make_async_copy(xs_hbm.at[at, :], xs.at[at, :], sems.at[0, i]),
                pltpu.make_async_copy(dxs_hbm.at[at, :], dxs.at[at, :], sems.at[1, i]),
            ]
        )
    copies[0][0].start()
    copies[0][1].start()
    b_copy.start()
    for pair_copies in copies[1:]:
        for copy in pair_copies:
            copy.start()
    bias = column_of([dt_bias[h] for h in range(heads)])
    rate = column_of([a_rate[h] * LOG2E for h in range(heads)])
    dt_copy.wait()
    raw = jnp.concatenate([dt_raw[...], jnp.zeros((PACK - heads, blocks * Q), F32)], axis=0)
    pre = jnp.concatenate([raw[:, c * Q : (c + 1) * Q] for c in range(blocks)], axis=0)
    pre = pre + jnp.concatenate([bias] * blocks, axis=0)
    step = jnp.maximum(pre, 0.0) + jnp.log1p(jnp.exp(-jnp.abs(pre)))
    upper = (
        lax.broadcasted_iota(jnp.int32, (Q, Q), 0) <= lax.broadcasted_iota(jnp.int32, (Q, Q), 1)
    ).astype(BF16)
    logs = jnp.zeros((blocks * PACK, Q), F32)
    for piece in split_bf16(-(step * jnp.concatenate([rate] * blocks, axis=0)), 3)[::-1]:
        logs = logs + jnp.dot(piece, upper, preferred_element_type=F32)
    shifted = logs - jnp.log2(step)
    shifted_out[...] = shifted
    logs_out[...] = logs
    ends = logs[:, Q - 1 : Q]
    weight_in = jnp.exp2(ends - shifted)
    end_decay = jnp.exp2(ends)

    factor = jnp.ones((PACK, 1), F32)
    keeps = [None]
    for c in range(blocks):
        if c > 0:
            keeps.append(jnp.where(traj[c] == traj[c - 1], 1.0, 0.0))
            factor = factor * keeps[c]
        fin[c * PACK : (c + 1) * PACK, :] = jnp.broadcast_to(factor, (PACK, LANES))
        factor = factor * end_decay[c * PACK : (c + 1) * PACK, :]
    copies_out = []
    b_copy.wait()
    for i, at in enumerate(chunks):
        for copy in copies[i]:
            copy.wait()
        members = [h for h in range(2 * i, min(2 * i + 2, heads))] * 2
        place = slice(2 * at.start, 2 * at.stop)
        state = jnp.zeros((len(members) * width, LANES), F32)
        for c in range(blocks):
            here = slice(c * Q, (c + 1) * Q)
            if c > 0:
                state = state * keeps[c]
            local_in[c, place, :] = state.astype(BF16)
            both = jnp.concatenate([xs[at, here], dxs[at, here]], axis=0).astype(F32)
            scale = jnp.concatenate(
                [
                    jnp.broadcast_to(
                        weight_in[c * PACK + h : c * PACK + h + 1, :], (width, Q)
                    )
                    for h in members
                ],
                axis=0,
            )
            gained = jnp.dot(
                (both * scale).astype(BF16), bmat[here, :], preferred_element_type=F32
            )
            decay = jnp.concatenate(
                [
                    jnp.broadcast_to(
                        end_decay[c * PACK + h : c * PACK + h + 1, :], (width, LANES)
                    )
                    for h in members
                ],
                axis=0,
            )
            state = state * decay + gained
        rows = pl.ds(place.start, place.stop - place.start)
        leaving = pltpu.make_async_copy(
            local_in.at[:, rows, :], local_out.at[:, rows, :], out_sems.at[i]
        )
        leaving.start()
        copies_out.append(leaving)
        send[:, place] = state.T.astype(BF16)
    lane = lax.broadcasted_iota(jnp.int32, (1, LANES), 1)
    notes = jnp.zeros((1, LANES), F32)
    for h in range(heads):
        rest = factor[h : h + 1, :]
        for k in range(3):
            piece = rest.astype(BF16).astype(F32)
            notes = jnp.where(lane == k * heads + h, piece, notes)
            rest = rest - piece
    notes = jnp.where(lane == 3 * heads, traj[0].astype(F32), notes)
    notes = jnp.where(lane == 3 * heads + 1, traj[blocks - 1].astype(F32), notes)
    send[:, heads * LANES :] = jnp.broadcast_to(notes, (LANES, LANES)).astype(BF16)
    for leaving in copies_out:
        leaving.wait()


def scan_kernel(heads, count, got, _, back, hold):
    width = heads * LANES
    everything = got[...].astype(F32)
    carried = jnp.zeros((PACK, width), F32)
    last_id = None
    for s in range(count):
        at = slice(s * PACK, (s + 1) * PACK)
        notes = everything[at, width:]
        factor = []
        for h in range(heads):
            total = notes[:, h : h + 1]
            for k in range(1, 3):
                total = total + notes[:, k * heads + h : k * heads + h + 1]
            factor.append(total)
        first_id = notes[:, 3 * heads : 3 * heads + 1]
        if s > 0:
            carried = jnp.where(first_id == last_id, carried, 0.0)
        hold[at, :] = carried
        last_id = notes[:, 3 * heads + 1 : 3 * heads + 2]
        carried = jnp.concatenate(by_head(factor, PACK), axis=1) * carried + everything[at, :width]
    back[...] = hold[...].astype(BF16)


def diagonal_kernel(
    heads, d_skip, xs, dxs, zgate, bmat, cmat, shifted, logs, local_in, fin, base, slope
):
    width = xs.shape[0] // heads
    block = pl.program_id(0)
    mine = pl.ds(pl.multiple_of(block * PACK, PACK), PACK)
    log_rows, shifted_rows = logs[mine, :], shifted[mine, :]
    table = jnp.concatenate([log_rows, jnp.zeros((LANES - PACK, Q), F32)], axis=0).T
    log_wide = [jnp.broadcast_to(table[:, h : h + 1], (Q, LANES)) for h in range(heads)]
    decays = [jnp.exp2(wide) for wide in log_wide]
    through = fin[mine, 0:1]
    scores = across(cmat[...], bmat[...])
    causal = lax.broadcasted_iota(jnp.int32, (HALF, HALF), 0) >= lax.broadcasted_iota(
        jnp.int32, (HALF, HALF), 1
    )
    unit = (
        lax.broadcasted_iota(jnp.int32, (Q, Q), 0) == lax.broadcasted_iota(jnp.int32, (Q, Q), 1)
    ).astype(BF16)
    nothing = jnp.zeros((HALF, HALF), BF16)
    z = across(unit, zgate[...])
    gate = z * (0.5 + 0.5 * jnp.tanh(0.5 * z))
    gate_last = gate[:, 2 * LANES :]
    gates = [
        gate[:, :LANES],
        gate[:, LANES : 2 * LANES],
        jnp.concatenate([gate_last, gate_last], axis=1),
    ]
    low = lax.broadcasted_iota(jnp.int32, (Q, LANES), 1) < LANES // 2

    def weights(h):
        log_t = log_wide[h]
        log_s = shifted_rows[h : h + 1, :]
        near = scores[:HALF, :HALF] * jnp.exp2(log_t[:HALF] - log_s[:, :HALF])
        far = scores[HALF:, :HALF] * jnp.exp2(log_t[HALF:] - log_s[:, :HALF])
        last = scores[HALF:, HALF:] * jnp.exp2(log_t[HALF:] - log_s[:, HALF:])
        top = jnp.concatenate([jnp.where(causal, near, 0.0).astype(BF16), nothing], axis=1)
        bottom = jnp.concatenate([far, jnp.where(causal, last, 0.0)], axis=1).astype(BF16)
        return [top, bottom]

    carried = across(cmat[...], local_in[0])
    factors = [through[h : h + 1, :] for h in range(heads)]
    skip = by_head([d_skip[h] for h in range(heads)], 1)
    rows = feature_rows(xs[...], dxs[...], heads, width)
    for pair in range(0, heads, 2):
        members = range(pair, min(pair + 2, heads))
        operand = jnp.concatenate([part for h, part in rows if h in members], axis=0)
        left = [piece for h in members for piece in weights(h)] + [unit]
        sums = across(jnp.concatenate(left, axis=0), operand)
        count = len(members)
        decay, factor = decays[pair], factors[pair]
        if count == 2:
            decay = jnp.where(low, decay, decays[pair + 1])
            factor = jnp.where(low, factor, factors[pair + 1])
        for i in range(count):
            tile = pair + i
            at = slice(tile * LANES, (tile + 1) * LANES)
            lanes = slice(i * LANES, (i + 1) * LANES)
            diagonal = sums[:Q, lanes]
            if count == 2:
                diagonal = jnp.where(low, diagonal, sums[Q : 2 * Q, lanes])
            plain = sums[count * Q :, lanes]
            y = diagonal + carried[:, at] * decay + plain * skip[tile]
            base[:, at] = (y * gates[pair // 2]).astype(BF16)
        at = slice(pair // 2 * LANES, (pair // 2 + 1) * LANES)
        slope[:, at] = (decay * factor * gates[pair // 2]).astype(BF16)


def gate_kernel(blocks, heads, base, slope, cmat, incoming, out):
    state = incoming[...]
    for c in range(blocks):
        here = slice(c * Q, (c + 1) * Q)
        carried = jnp.dot(cmat[here, :], state, preferred_element_type=F32)
        for i in range(heads):
            at = slice(i * LANES, (i + 1) * LANES)
            gain = slope[here, i // 2 * LANES : (i // 2 + 1) * LANES].astype(F32)
            out[here, at] = (base[here, at].astype(F32) + carried[:, at] * gain).astype(BF16)


def norm_kernel(
    heads, sources, strip, strips, total_width, gathered, gain, normed, normed_tan, held, sems
):
    half = LANES // 2
    width = heads * half
    copies = []
    for r in range(strips):
        here = slice(r * strip, (r + 1) * strip)
        main_parts, tan_parts = [], []
        for s in range(sources):
            tiles = [
                gathered[s, here, i * LANES : (i + 1) * LANES].astype(F32) for i in range(heads)
            ]
            main_parts += [tiles[0], tiles[2], tiles[4][:, :half]]
            tan_parts += [tiles[1], tiles[3], tiles[4][:, half:]]
        mains, tans = [], []
        for s in range(0, sources, 2):
            mains.append(jnp.concatenate(main_parts[3 * s : 3 * s + 6], axis=1))
            tans.append(jnp.concatenate(tan_parts[3 * s : 3 * s + 6], axis=1))
        square = sum(m * m for m in mains)
        cross = sum(m * t for m, t in zip(mains, tans))
        mean_square = jnp.sum(square, axis=1, keepdims=True) / total_width
        mean_cross = jnp.sum(cross, axis=1, keepdims=True) / total_width
        inv_rms = lax.rsqrt(mean_square + 1e-05)
        pull = inv_rms * inv_rms * inv_rms * mean_cross
        for i, (m, t) in enumerate(zip(mains, tans)):
            at = slice(i * 2 * width, (i + 1) * 2 * width)
            g = gain[:, at]
            held[0, here, at] = (g * m * inv_rms).astype(BF16)
            held[1, here, at] = (g * (t * inv_rms - m * pull)).astype(BF16)
        for k, target in enumerate((normed, normed_tan)):
            copy = pltpu.make_async_copy(held.at[k, here, :], target.at[here, :], sems.at[k, r])
            copy.start()
            copies.append(copy)
    for copy in copies:
        copy.wait()


def whole(shape):
    return pl.BlockSpec(shape, lambda *_: (0,) * len(shape))


SMEM_SPEC = pl.BlockSpec(memory_space=pltpu.SMEM)


def local(xs, dxs, zgate, bmat, cmat, dt_raw, dt_bias, a_rate, d_skip, gain, traj_ids):
    tokens, inner = xs.shape
    heads = dt_raw.shape[0]
    blocks = tokens // Q
    wide = heads * LANES
    state_rows = bmat.shape[1]
    sources = lax.axis_size("head")
    seq_size = lax.axis_size("seq")
    group = state_rows // PACK
    groups = [list(range(g, g + group)) for g in range(0, seq_size, group)]
    params = pltpu.CompilerParams(vmem_limit_bytes=60 * MIB)
    roomy = pltpu.CompilerParams(vmem_limit_bytes=32 * MIB)
    small = pltpu.CompilerParams(vmem_limit_bytes=16 * MIB)
    in_vmem = pl.BlockSpec(memory_space=pltpu.VMEM)
    in_hbm = pl.BlockSpec(memory_space=pl.ANY)
    c_plain = cmat
    xs, dxs, zgate, bmat, cmat, dt_raw = [
        pltpu.with_memory_space_constraint(array, pltpu.HBM)
        for array in (xs.T, dxs.T, zgate.T, bmat, cmat, dt_raw)
    ]

    def pinned(array):
        return pltpu.with_memory_space_constraint(array, pltpu.VMEM)

    shifted, logs, local_in, fin, send = pl.pallas_call(
        functools.partial(state_kernel, heads, blocks),
        out_shape=(
            pltpu.VMEM((blocks * PACK, Q), F32),
            pltpu.VMEM((blocks * PACK, Q), F32),
            jax.ShapeDtypeStruct((blocks, wide, state_rows), BF16),
            pltpu.VMEM((blocks * PACK, LANES), F32),
            pltpu.VMEM((state_rows, wide + LANES), BF16),
        ),
        in_specs=[SMEM_SPEC] * 3 + [in_hbm] * 4,
        out_specs=(in_vmem, in_vmem, in_hbm, in_vmem, in_vmem),
        scratch_shapes=[
            pltpu.VMEM((inner, tokens), BF16),
            pltpu.VMEM((inner, tokens), BF16),
            pltpu.VMEM((tokens, state_rows), BF16),
            pltpu.VMEM((blocks, wide, state_rows), BF16),
            pltpu.VMEM((heads, tokens), F32),
            pltpu.SemaphoreType.DMA((3, len(range(0, heads, 2)))),
            pltpu.SemaphoreType.DMA((len(range(0, heads, 2)),)),
        ],
        compiler_params=params,
        cost_estimate=pl.CostEstimate(
            flops=300_000_000, bytes_accessed=4_000_000, transcendentals=30_000
        ),
    )(dt_bias, a_rate, traj_ids, dt_raw, xs, dxs, bmat)

    def token_block(width):
        return pl.BlockSpec((Q, width), lambda c: (c, 0))

    def feature_block(width):
        return pl.BlockSpec((width, Q), lambda c: (0, c))

    lean = (heads + 1) // 2 * LANES
    base, slope = pl.pallas_call(
        functools.partial(diagonal_kernel, heads),
        grid=(blocks,),
        out_shape=(
            pltpu.VMEM((tokens, wide), BF16),
            pltpu.VMEM((tokens, lean), BF16),
        ),
        in_specs=[
            SMEM_SPEC,
            feature_block(inner),
            feature_block(inner),
            feature_block(inner),
            token_block(state_rows),
            token_block(state_rows),
            in_vmem,
            in_vmem,
            pl.BlockSpec((1, wide, state_rows), lambda c: (c, 0, 0)),
            in_vmem,
        ],
        out_specs=(token_block(wide), token_block(lean)),
        compiler_params=roomy,
        cost_estimate=pl.CostEstimate(
            flops=2_000_000_000, bytes_accessed=16_000_000, transcendentals=2_000_000
        ),
    )(
        d_skip,
        xs,
        dxs,
        zgate,
        bmat,
        cmat,
        pinned(shifted),
        pinned(logs),
        pltpu.with_memory_space_constraint(local_in, pltpu.HBM),
        pinned(fin),
    )

    got = lax.all_to_all(
        send, "seq", split_axis=0, concat_axis=0, tiled=True, axis_index_groups=groups
    )
    back = pl.pallas_call(
        functools.partial(scan_kernel, heads, group),
        out_shape=jax.ShapeDtypeStruct((state_rows, wide), BF16),
        in_specs=[in_vmem, in_hbm],
        scratch_shapes=[pltpu.VMEM((state_rows, wide), F32)],
        compiler_params=small,
    )(got, pinned(slope))
    incoming = lax.all_to_all(
        back, "seq", split_axis=0, concat_axis=0, tiled=True, axis_index_groups=groups
    )
    gated = pl.pallas_call(
        functools.partial(gate_kernel, blocks, heads),
        out_shape=jax.ShapeDtypeStruct((tokens, wide), BF16),
        in_specs=[in_vmem] * 4,
        compiler_params=small,
        cost_estimate=pl.CostEstimate(
            flops=260_000_000, bytes_accessed=6_000_000, transcendentals=0
        ),
    )(
        pinned(base),
        pinned(slope),
        pinned(c_plain),
        incoming,
    )

    gathered = lax.all_to_all(gated, "head", split_axis=0, concat_axis=0, tiled=True)
    mine = tokens // sources
    strip = 16
    strips = mine // strip
    total = inner * sources
    return pl.pallas_call(
        functools.partial(norm_kernel, heads, sources, strip, strips, float(total)),
        out_shape=(
            jax.ShapeDtypeStruct((mine, total), BF16),
            jax.ShapeDtypeStruct((mine, total), BF16),
        ),
        in_specs=[in_vmem] * 2,
        out_specs=(in_hbm, in_hbm),
        scratch_shapes=[
            pltpu.VMEM((2, mine, total), BF16),
            pltpu.SemaphoreType.DMA((2, strips)),
        ],
        compiler_params=small,
    )(gathered.reshape(sources, mine, wide), gain.reshape(1, total))


def solution(mesh):
    placed = (
        P("seq", "head"),
        P("seq", "head"),
        P("seq", "head"),
        P("seq", None),
        P("seq", None),
        P("head", "seq"),
        P("head"),
        P("head"),
        P("head"),
        P(),
        P("seq"),
    )
    return jax.shard_map(
        local,
        mesh=mesh,
        in_specs=placed,
        out_specs=(P(("seq", "head"), None), P(("seq", "head"), None)),
        check_vma=False,
    )
```

```python
import functools

import jax
import jax.numpy as jnp
from jax import lax
from jax.experimental import pallas as pl
from jax.experimental.pallas import tpu as pltpu
from jax.sharding import PartitionSpec as P

Q = 256
HALF = 128
LANES = 128
PACK = 8
MIB = 1024 * 1024
F32 = jnp.float32
BF16 = jnp.bfloat16


def column_of(values):
    place = lax.broadcasted_iota(jnp.int32, (PACK, 1), 0)
    column = jnp.zeros((PACK, 1), F32)
    for h, value in enumerate(values):
        column = jnp.where(place == h, value, column)
    return column


def by_head(per_head, rows):
    low = lax.broadcasted_iota(jnp.int32, (rows, LANES), 1) < LANES // 2
    first = jnp.where(low, per_head[0], per_head[1])
    second = jnp.where(low, per_head[2], per_head[3])
    last = jnp.broadcast_to(per_head[4], (rows, LANES))
    return [first, first, second, second, last]


def feature_rows(main, tan, heads, width):
    order = []
    for pair in range(0, heads, 2):
        for array in (main, tan):
            for h in range(pair, min(pair + 2, heads)):
                order.append((h, array[h * width : (h + 1) * width, :]))
    return order


def split_bf16(x, parts):
    pieces = []
    for _ in range(parts):
        piece = x.astype(BF16)
        pieces.append(piece)
        x = x - piece.astype(F32)
    return pieces


def across(left, right):
    return lax.dot_general(left, right, (((1,), (1,)), ((), ())), preferred_element_type=F32)


def state_kernel(
    heads,
    blocks,
    bias_hbm,
    rate_hbm,
    traj_hbm,
    dt_hbm,
    xs_hbm,
    dxs_hbm,
    bmat_hbm,
    shifted_out,
    logs_out,
    local_out,
    fin,
    send,
    xs,
    dxs,
    bmat,
    local_in,
    dt_raw,
    dt_bias,
    a_rate,
    traj,
    sems,
    out_sems,
    small_sems,
):
    width = xs.shape[0] // heads
    chunks = [slice(h * width, min(h + 2, heads) * width) for h in range(0, heads, 2)]
    b_copy = pltpu.make_async_copy(bmat_hbm, bmat, sems.at[2, 0])
    dt_copy = pltpu.make_async_copy(dt_hbm, dt_raw, sems.at[2, 1])
    dt_copy.start()
    copies = []
    for i, at in enumerate(chunks):
        copies.append(
            [
                pltpu.make_async_copy(xs_hbm.at[at, :], xs.at[at, :], sems.at[0, i]),
                pltpu.make_async_copy(dxs_hbm.at[at, :], dxs.at[at, :], sems.at[1, i]),
            ]
        )
    copies[0][0].start()
    copies[0][1].start()
    b_copy.start()
    small_copies = [
        pltpu.make_async_copy(source, target, small_sems.at[i])
        for i, (source, target) in enumerate(
            ((bias_hbm, dt_bias), (rate_hbm, a_rate), (traj_hbm, traj))
        )
    ]
    for copy in small_copies:
        copy.start()
    for pair_copies in copies[1:]:
        for copy in pair_copies:
            copy.start()
    for copy in small_copies:
        copy.wait()
    bias = column_of([dt_bias[h] for h in range(heads)])
    rate = column_of([a_rate[h] for h in range(heads)])
    dt_copy.wait()
    raw = jnp.concatenate([dt_raw[...], jnp.zeros((PACK - heads, blocks * Q), F32)], axis=0)
    pre = jnp.concatenate([raw[:, c * Q : (c + 1) * Q] for c in range(blocks)], axis=0)
    pre = pre + jnp.concatenate([bias] * blocks, axis=0)
    step = jnp.maximum(pre, 0.0) + jnp.log1p(jnp.exp(-jnp.abs(pre)))
    upper = (
        lax.broadcasted_iota(jnp.int32, (Q, Q), 0) <= lax.broadcasted_iota(jnp.int32, (Q, Q), 1)
    ).astype(BF16)
    logs = jnp.zeros((blocks * PACK, Q), F32)
    for piece in split_bf16(-(step * jnp.concatenate([rate] * blocks, axis=0)), 3)[::-1]:
        logs = logs + jnp.dot(piece, upper, preferred_element_type=F32)
    shifted = logs - jnp.log(step)
    shifted_out[...] = shifted
    logs_out[...] = logs
    ends = logs[:, Q - 1 : Q]
    weight_in = jnp.exp(ends - shifted)
    end_decay = jnp.exp(ends)

    factor = jnp.ones((PACK, 1), F32)
    keeps = [None]
    for c in range(blocks):
        if c > 0:
            keeps.append(jnp.where(traj[c] == traj[c - 1], 1.0, 0.0))
            factor = factor * keeps[c]
        fin[c * PACK : (c + 1) * PACK, :] = jnp.broadcast_to(factor, (PACK, LANES))
        factor = factor * end_decay[c * PACK : (c + 1) * PACK, :]
    copies_out = []
    b_copy.wait()
    for i, at in enumerate(chunks):
        for copy in copies[i]:
            copy.wait()
        members = [h for h in range(2 * i, min(2 * i + 2, heads))] * 2
        place = slice(2 * at.start, 2 * at.stop)
        state = jnp.zeros((len(members) * width, LANES), F32)
        for c in range(blocks):
            here = slice(c * Q, (c + 1) * Q)
            if c > 0:
                state = state * keeps[c]
            local_in[c, place, :] = state.astype(BF16)
            both = jnp.concatenate([xs[at, here], dxs[at, here]], axis=0).astype(F32)
            scale = jnp.concatenate(
                [
                    jnp.broadcast_to(
                        weight_in[c * PACK + h : c * PACK + h + 1, :], (width, Q)
                    )
                    for h in members
                ],
                axis=0,
            )
            gained = jnp.dot(
                (both * scale).astype(BF16), bmat[here, :], preferred_element_type=F32
            )
            decay = jnp.concatenate(
                [
                    jnp.broadcast_to(
                        end_decay[c * PACK + h : c * PACK + h + 1, :], (width, LANES)
                    )
                    for h in members
                ],
                axis=0,
            )
            state = state * decay + gained
        rows = pl.ds(place.start, place.stop - place.start)
        leaving = pltpu.make_async_copy(
            local_in.at[:, rows, :], local_out.at[:, rows, :], out_sems.at[i]
        )
        leaving.start()
        copies_out.append(leaving)
        send[:, place] = state.T.astype(BF16)
    lane = lax.broadcasted_iota(jnp.int32, (1, LANES), 1)
    notes = jnp.zeros((1, LANES), F32)
    for h in range(heads):
        rest = factor[h : h + 1, :]
        for k in range(3):
            piece = rest.astype(BF16).astype(F32)
            notes = jnp.where(lane == k * heads + h, piece, notes)
            rest = rest - piece
    notes = jnp.where(lane == 3 * heads, traj[0].astype(F32), notes)
    notes = jnp.where(lane == 3 * heads + 1, traj[blocks - 1].astype(F32), notes)
    send[:, heads * LANES :] = jnp.broadcast_to(notes, (LANES, LANES)).astype(BF16)
    for leaving in copies_out:
        leaving.wait()


def scan_kernel(heads, count, got, _, back, hold):
    width = heads * LANES
    everything = got[...].astype(F32)
    carried = jnp.zeros((PACK, width), F32)
    last_id = None
    for s in range(count):
        at = slice(s * PACK, (s + 1) * PACK)
        notes = everything[at, width:]
        factor = []
        for h in range(heads):
            total = notes[:, h : h + 1]
            for k in range(1, 3):
                total = total + notes[:, k * heads + h : k * heads + h + 1]
            factor.append(total)
        first_id = notes[:, 3 * heads : 3 * heads + 1]
        if s > 0:
            carried = jnp.where(first_id == last_id, carried, 0.0)
        hold[at, :] = carried
        last_id = notes[:, 3 * heads + 1 : 3 * heads + 2]
        carried = jnp.concatenate(by_head(factor, PACK), axis=1) * carried + everything[at, :width]
    back[...] = hold[...].astype(BF16)


def diagonal_kernel(
    heads, d_skip, xs, dxs, zgate, bmat, cmat, shifted, logs, local_in, fin, base, slope
):
    width = xs.shape[0] // heads
    block = pl.program_id(0)
    mine = pl.ds(pl.multiple_of(block * PACK, PACK), PACK)
    log_rows, shifted_rows = logs[mine, :], shifted[mine, :]
    table = jnp.concatenate([log_rows, jnp.zeros((LANES - PACK, Q), F32)], axis=0).T
    log_wide = [jnp.broadcast_to(table[:, h : h + 1], (Q, LANES)) for h in range(heads)]
    decays = [jnp.exp(wide) for wide in log_wide]
    through = fin[mine, 0:1]
    scores = across(cmat[...], bmat[...])
    causal = lax.broadcasted_iota(jnp.int32, (HALF, HALF), 0) >= lax.broadcasted_iota(
        jnp.int32, (HALF, HALF), 1
    )
    unit = (
        lax.broadcasted_iota(jnp.int32, (Q, Q), 0) == lax.broadcasted_iota(jnp.int32, (Q, Q), 1)
    ).astype(BF16)
    nothing = jnp.zeros((HALF, HALF), BF16)
    z = across(unit, zgate[...])
    gate = z * (0.5 + 0.5 * jnp.tanh(0.5 * z))
    gate_last = gate[:, 2 * LANES :]
    gates = [
        gate[:, :LANES],
        gate[:, LANES : 2 * LANES],
        jnp.concatenate([gate_last, gate_last], axis=1),
    ]
    low = lax.broadcasted_iota(jnp.int32, (Q, LANES), 1) < LANES // 2

    def weights(h):
        log_t = log_wide[h]
        log_s = shifted_rows[h : h + 1, :]
        near = scores[:HALF, :HALF] * jnp.exp(log_t[:HALF] - log_s[:, :HALF])
        far = scores[HALF:, :HALF] * jnp.exp(log_t[HALF:] - log_s[:, :HALF])
        last = scores[HALF:, HALF:] * jnp.exp(log_t[HALF:] - log_s[:, HALF:])
        top = jnp.concatenate([jnp.where(causal, near, 0.0).astype(BF16), nothing], axis=1)
        bottom = jnp.concatenate([far, jnp.where(causal, last, 0.0)], axis=1).astype(BF16)
        return [top, bottom]

    carried = across(cmat[...], local_in[0])
    factors = [through[h : h + 1, :] for h in range(heads)]
    skip = by_head([d_skip[h] for h in range(heads)], 1)
    rows = feature_rows(xs[...], dxs[...], heads, width)
    for pair in range(0, heads, 2):
        members = range(pair, min(pair + 2, heads))
        operand = jnp.concatenate([part for h, part in rows if h in members], axis=0)
        left = [piece for h in members for piece in weights(h)] + [unit]
        sums = across(jnp.concatenate(left, axis=0), operand)
        count = len(members)
        decay, factor = decays[pair], factors[pair]
        if count == 2:
            decay = jnp.where(low, decay, decays[pair + 1])
            factor = jnp.where(low, factor, factors[pair + 1])
        for i in range(count):
            tile = pair + i
            at = slice(tile * LANES, (tile + 1) * LANES)
            lanes = slice(i * LANES, (i + 1) * LANES)
            diagonal = sums[:Q, lanes]
            if count == 2:
                diagonal = jnp.where(low, diagonal, sums[Q : 2 * Q, lanes])
            plain = sums[count * Q :, lanes]
            y = diagonal + carried[:, at] * decay + plain * skip[tile]
            base[:, at] = (y * gates[pair // 2]).astype(BF16)
        at = slice(pair // 2 * LANES, (pair // 2 + 1) * LANES)
        slope[:, at] = (decay * factor * gates[pair // 2]).astype(BF16)


def gate_kernel(blocks, heads, base, slope, cmat, incoming, out):
    state = incoming[...]
    for c in range(blocks):
        here = slice(c * Q, (c + 1) * Q)
        carried = jnp.dot(cmat[here, :], state, preferred_element_type=F32)
        for i in range(heads):
            at = slice(i * LANES, (i + 1) * LANES)
            gain = slope[here, i // 2 * LANES : (i // 2 + 1) * LANES].astype(F32)
            out[here, at] = (base[here, at].astype(F32) + carried[:, at] * gain).astype(BF16)


def norm_kernel(
    heads, sources, strip, strips, total_width, gathered, gain, normed, normed_tan, held, sems
):
    half = LANES // 2
    width = heads * half
    copies = []
    for r in range(strips):
        here = slice(r * strip, (r + 1) * strip)
        main_parts, tan_parts = [], []
        for s in range(sources):
            tiles = [
                gathered[s, here, i * LANES : (i + 1) * LANES].astype(F32) for i in range(heads)
            ]
            main_parts += [tiles[0], tiles[2], tiles[4][:, :half]]
            tan_parts += [tiles[1], tiles[3], tiles[4][:, half:]]
        mains, tans = [], []
        for s in range(0, sources, 2):
            mains.append(jnp.concatenate(main_parts[3 * s : 3 * s + 6], axis=1))
            tans.append(jnp.concatenate(tan_parts[3 * s : 3 * s + 6], axis=1))
        square = sum(m * m for m in mains)
        cross = sum(m * t for m, t in zip(mains, tans))
        mean_square = jnp.sum(square, axis=1, keepdims=True) / total_width
        mean_cross = jnp.sum(cross, axis=1, keepdims=True) / total_width
        inv_rms = lax.rsqrt(mean_square + 1e-05)
        pull = inv_rms * inv_rms * inv_rms * mean_cross
        for i, (m, t) in enumerate(zip(mains, tans)):
            at = slice(i * 2 * width, (i + 1) * 2 * width)
            g = gain[:, at]
            held[0, here, at] = (g * m * inv_rms).astype(BF16)
            held[1, here, at] = (g * (t * inv_rms - m * pull)).astype(BF16)
        for k, target in enumerate((normed, normed_tan)):
            copy = pltpu.make_async_copy(held.at[k, here, :], target.at[here, :], sems.at[k, r])
            copy.start()
            copies.append(copy)
    for copy in copies:
        copy.wait()


def whole(shape):
    return pl.BlockSpec(shape, lambda *_: (0,) * len(shape))


SMEM_SPEC = pl.BlockSpec(memory_space=pltpu.SMEM)


def local(xs, dxs, zgate, bmat, cmat, dt_raw, dt_bias, a_rate, d_skip, gain, traj_ids):
    tokens, inner = xs.shape
    heads = dt_raw.shape[0]
    blocks = tokens // Q
    wide = heads * LANES
    state_rows = bmat.shape[1]
    sources = lax.axis_size("head")
    seq_size = lax.axis_size("seq")
    group = state_rows // PACK
    groups = [list(range(g, g + group)) for g in range(0, seq_size, group)]
    params = pltpu.CompilerParams(vmem_limit_bytes=60 * MIB)
    roomy = pltpu.CompilerParams(vmem_limit_bytes=32 * MIB)
    small = pltpu.CompilerParams(vmem_limit_bytes=16 * MIB)
    in_vmem = pl.BlockSpec(memory_space=pltpu.VMEM)
    in_hbm = pl.BlockSpec(memory_space=pl.ANY)
    c_plain = cmat
    xs, dxs, zgate, bmat, cmat, dt_raw = [
        pltpu.with_memory_space_constraint(array, pltpu.HBM)
        for array in (xs.T, dxs.T, zgate.T, bmat, cmat, dt_raw)
    ]

    def pinned(array):
        return pltpu.with_memory_space_constraint(array, pltpu.VMEM)

    shifted, logs, local_in, fin, send = pl.pallas_call(
        functools.partial(state_kernel, heads, blocks),
        out_shape=(
            pltpu.VMEM((blocks * PACK, Q), F32),
            pltpu.VMEM((blocks * PACK, Q), F32),
            jax.ShapeDtypeStruct((blocks, wide, state_rows), BF16),
            pltpu.VMEM((blocks * PACK, LANES), F32),
            pltpu.VMEM((state_rows, wide + LANES), BF16),
        ),
        in_specs=[in_hbm] * 7,
        out_specs=(in_vmem, in_vmem, in_hbm, in_vmem, in_vmem),
        scratch_shapes=[
            pltpu.VMEM((inner, tokens), BF16),
            pltpu.VMEM((inner, tokens), BF16),
            pltpu.VMEM((tokens, state_rows), BF16),
            pltpu.VMEM((blocks, wide, state_rows), BF16),
            pltpu.VMEM((heads, tokens), F32),
            pltpu.SMEM((heads,), F32),
            pltpu.SMEM((heads,), F32),
            pltpu.SMEM((blocks,), jnp.int32),
            pltpu.SemaphoreType.DMA((3, len(range(0, heads, 2)))),
            pltpu.SemaphoreType.DMA((len(range(0, heads, 2)),)),
            pltpu.SemaphoreType.DMA((3,)),
        ],
        compiler_params=params,
        cost_estimate=pl.CostEstimate(
            flops=300_000_000, bytes_accessed=4_000_000, transcendentals=30_000
        ),
    )(dt_bias, a_rate, traj_ids, dt_raw, xs, dxs, bmat)

    def token_block(width):
        return pl.BlockSpec((Q, width), lambda c: (c, 0))

    def feature_block(width):
        return pl.BlockSpec((width, Q), lambda c: (0, c))

    lean = (heads + 1) // 2 * LANES
    base, slope = pl.pallas_call(
        functools.partial(diagonal_kernel, heads),
        grid=(blocks,),
        out_shape=(
            pltpu.VMEM((tokens, wide), BF16),
            pltpu.VMEM((tokens, lean), BF16),
        ),
        in_specs=[
            SMEM_SPEC,
            feature_block(inner),
            feature_block(inner),
            feature_block(inner),
            token_block(state_rows),
            token_block(state_rows),
            in_vmem,
            in_vmem,
            pl.BlockSpec((1, wide, state_rows), lambda c: (c, 0, 0)),
            in_vmem,
        ],
        out_specs=(token_block(wide), token_block(lean)),
        compiler_params=roomy,
        cost_estimate=pl.CostEstimate(
            flops=2_000_000_000, bytes_accessed=16_000_000, transcendentals=2_000_000
        ),
    )(
        d_skip,
        xs,
        dxs,
        zgate,
        bmat,
        cmat,
        pinned(shifted),
        pinned(logs),
        pltpu.with_memory_space_constraint(local_in, pltpu.HBM),
        pinned(fin),
    )

    got = lax.all_to_all(
        send, "seq", split_axis=0, concat_axis=0, tiled=True, axis_index_groups=groups
    )
    back = pl.pallas_call(
        functools.partial(scan_kernel, heads, group),
        out_shape=jax.ShapeDtypeStruct((state_rows, wide), BF16),
        in_specs=[in_vmem, in_hbm],
        scratch_shapes=[pltpu.VMEM((state_rows, wide), F32)],
        compiler_params=small,
    )(got, pinned(slope))
    incoming = lax.all_to_all(
        back, "seq", split_axis=0, concat_axis=0, tiled=True, axis_index_groups=groups
    )
    gated = pl.pallas_call(
        functools.partial(gate_kernel, blocks, heads),
        out_shape=jax.ShapeDtypeStruct((tokens, wide), BF16),
        in_specs=[in_vmem] * 4,
        compiler_params=small,
        cost_estimate=pl.CostEstimate(
            flops=260_000_000, bytes_accessed=6_000_000, transcendentals=0
        ),
    )(
        pinned(base),
        pinned(slope),
        pinned(c_plain),
        incoming,
    )

    gathered = lax.all_to_all(gated, "head", split_axis=0, concat_axis=0, tiled=True)
    mine = tokens // sources
    strip = 16
    strips = mine // strip
    total = inner * sources
    return pl.pallas_call(
        functools.partial(norm_kernel, heads, sources, strip, strips, float(total)),
        out_shape=(
            jax.ShapeDtypeStruct((mine, total), BF16),
            jax.ShapeDtypeStruct((mine, total), BF16),
        ),
        in_specs=[in_vmem] * 2,
        out_specs=(in_hbm, in_hbm),
        scratch_shapes=[
            pltpu.VMEM((2, mine, total), BF16),
            pltpu.SemaphoreType.DMA((2, strips)),
        ],
        compiler_params=small,
    )(gathered.reshape(sources, mine, wide), gain.reshape(1, total))


def solution(mesh):
    placed = (
        P("seq", "head"),
        P("seq", "head"),
        P("seq", "head"),
        P("seq", None),
        P("seq", None),
        P("head", "seq"),
        P("head"),
        P("head"),
        P("head"),
        P(),
        P("seq"),
    )
    return jax.shard_map(
        local,
        mesh=mesh,
        in_specs=placed,
        out_specs=(P(("seq", "head"), None), P(("seq", "head"), None)),
        check_vma=False,
    )
```

```python
import functools

import jax
import jax.numpy as jnp
from jax import lax
from jax.experimental import pallas as pl
from jax.experimental.pallas import tpu as pltpu
from jax.sharding import PartitionSpec as P

Q = 256
HALF = 128
LANES = 128
PACK = 8
MIB = 1024 * 1024
F32 = jnp.float32
BF16 = jnp.bfloat16


def column_of(values):
    place = lax.broadcasted_iota(jnp.int32, (PACK, 1), 0)
    column = jnp.zeros((PACK, 1), F32)
    for h, value in enumerate(values):
        column = jnp.where(place == h, value, column)
    return column


def by_head(per_head, rows):
    low = lax.broadcasted_iota(jnp.int32, (rows, LANES), 1) < LANES // 2
    first = jnp.where(low, per_head[0], per_head[1])
    second = jnp.where(low, per_head[2], per_head[3])
    last = jnp.broadcast_to(per_head[4], (rows, LANES))
    return [first, first, second, second, last]


def feature_rows(main, tan, heads, width):
    order = []
    for pair in range(0, heads, 2):
        for array in (main, tan):
            for h in range(pair, min(pair + 2, heads)):
                order.append((h, array[h * width : (h + 1) * width, :]))
    return order


def split_bf16(x, parts):
    pieces = []
    for _ in range(parts):
        piece = x.astype(BF16)
        pieces.append(piece)
        x = x - piece.astype(F32)
    return pieces


def across(left, right):
    return lax.dot_general(left, right, (((1,), (1,)), ((), ())), preferred_element_type=F32)


def state_kernel(
    heads,
    blocks,
    bias_hbm,
    rate_hbm,
    traj_hbm,
    dt_hbm,
    xs_hbm,
    dxs_hbm,
    bmat_hbm,
    shifted_out,
    logs_out,
    local_out,
    fin,
    send,
    xs,
    dxs,
    bmat,
    local_in,
    dt_raw,
    dt_bias,
    a_rate,
    traj,
    sems,
    out_sems,
    small_sems,
):
    width = xs.shape[0] // heads
    chunks = [slice(h * width, min(h + 2, heads) * width) for h in range(0, heads, 2)]
    b_copy = pltpu.make_async_copy(bmat_hbm, bmat, sems.at[2, 0])
    dt_copy = pltpu.make_async_copy(dt_hbm, dt_raw, sems.at[2, 1])
    dt_copy.start()
    head_rows = chunks[0].stop
    parts = [pl.ds(0, head_rows), pl.ds(head_rows, xs.shape[0] - head_rows)]
    copies = [
        [
            pltpu.make_async_copy(xs_hbm.at[part, :], xs.at[part, :], sems.at[0, i]),
            pltpu.make_async_copy(dxs_hbm.at[part, :], dxs.at[part, :], sems.at[1, i]),
        ]
        for i, part in enumerate(parts)
    ] + [[] for _ in chunks[2:]]
    for copy in copies[0] + [b_copy] + copies[1]:
        copy.start()
    small_copies = [
        pltpu.make_async_copy(source, target, small_sems.at[i])
        for i, (source, target) in enumerate(
            ((bias_hbm, dt_bias), (rate_hbm, a_rate), (traj_hbm, traj))
        )
    ]
    for copy in small_copies:
        copy.start()
    for copy in small_copies:
        copy.wait()
    bias = column_of([dt_bias[h] for h in range(heads)])
    rate = column_of([a_rate[h] for h in range(heads)])
    dt_copy.wait()
    raw = jnp.concatenate([dt_raw[...], jnp.zeros((PACK - heads, blocks * Q), F32)], axis=0)
    pre = jnp.concatenate([raw[:, c * Q : (c + 1) * Q] for c in range(blocks)], axis=0)
    pre = pre + jnp.concatenate([bias] * blocks, axis=0)
    step = jnp.maximum(pre, 0.0) + jnp.log1p(jnp.exp(-jnp.abs(pre)))
    upper = (
        lax.broadcasted_iota(jnp.int32, (Q, Q), 0) <= lax.broadcasted_iota(jnp.int32, (Q, Q), 1)
    ).astype(BF16)
    logs = jnp.zeros((blocks * PACK, Q), F32)
    for piece in split_bf16(-(step * jnp.concatenate([rate] * blocks, axis=0)), 3)[::-1]:
        logs = logs + jnp.dot(piece, upper, preferred_element_type=F32)
    shifted = logs - jnp.log(step)
    shifted_out[...] = shifted
    logs_out[...] = logs
    ends = logs[:, Q - 1 : Q]
    weight_in = jnp.exp(ends - shifted)
    end_decay = jnp.exp(ends)

    factor = jnp.ones((PACK, 1), F32)
    keeps = [None]
    for c in range(blocks):
        if c > 0:
            keeps.append(jnp.where(traj[c] == traj[c - 1], 1.0, 0.0))
            factor = factor * keeps[c]
        fin[c * PACK : (c + 1) * PACK, :] = jnp.broadcast_to(factor, (PACK, LANES))
        factor = factor * end_decay[c * PACK : (c + 1) * PACK, :]
    copies_out = []
    b_copy.wait()
    for i, at in enumerate(chunks):
        for copy in copies[i]:
            copy.wait()
        members = [h for h in range(2 * i, min(2 * i + 2, heads))] * 2
        place = slice(2 * at.start, 2 * at.stop)
        state = jnp.zeros((len(members) * width, LANES), F32)
        for c in range(blocks):
            here = slice(c * Q, (c + 1) * Q)
            if c > 0:
                state = state * keeps[c]
            local_in[c, place, :] = state.astype(BF16)
            both = jnp.concatenate([xs[at, here], dxs[at, here]], axis=0).astype(F32)
            scale = jnp.concatenate(
                [
                    jnp.broadcast_to(
                        weight_in[c * PACK + h : c * PACK + h + 1, :], (width, Q)
                    )
                    for h in members
                ],
                axis=0,
            )
            gained = jnp.dot(
                (both * scale).astype(BF16), bmat[here, :], preferred_element_type=F32
            )
            decay = jnp.concatenate(
                [
                    jnp.broadcast_to(
                        end_decay[c * PACK + h : c * PACK + h + 1, :], (width, LANES)
                    )
                    for h in members
                ],
                axis=0,
            )
            state = state * decay + gained
        rows = pl.ds(place.start, place.stop - place.start)
        leaving = pltpu.make_async_copy(
            local_in.at[:, rows, :], local_out.at[:, rows, :], out_sems.at[i]
        )
        leaving.start()
        copies_out.append(leaving)
        send[:, place] = state.T.astype(BF16)
    lane = lax.broadcasted_iota(jnp.int32, (1, LANES), 1)
    notes = jnp.zeros((1, LANES), F32)
    for h in range(heads):
        rest = factor[h : h + 1, :]
        for k in range(3):
            piece = rest.astype(BF16).astype(F32)
            notes = jnp.where(lane == k * heads + h, piece, notes)
            rest = rest - piece
    notes = jnp.where(lane == 3 * heads, traj[0].astype(F32), notes)
    notes = jnp.where(lane == 3 * heads + 1, traj[blocks - 1].astype(F32), notes)
    send[:, heads * LANES :] = jnp.broadcast_to(notes, (LANES, LANES)).astype(BF16)
    for leaving in copies_out:
        leaving.wait()


def scan_kernel(heads, count, got, _, back, hold):
    width = heads * LANES
    everything = got[...].astype(F32)
    carried = jnp.zeros((PACK, width), F32)
    last_id = None
    for s in range(count):
        at = slice(s * PACK, (s + 1) * PACK)
        notes = everything[at, width:]
        factor = []
        for h in range(heads):
            total = notes[:, h : h + 1]
            for k in range(1, 3):
                total = total + notes[:, k * heads + h : k * heads + h + 1]
            factor.append(total)
        first_id = notes[:, 3 * heads : 3 * heads + 1]
        if s > 0:
            carried = jnp.where(first_id == last_id, carried, 0.0)
        hold[at, :] = carried
        last_id = notes[:, 3 * heads + 1 : 3 * heads + 2]
        carried = jnp.concatenate(by_head(factor, PACK), axis=1) * carried + everything[at, :width]
    back[...] = hold[...].astype(BF16)


def diagonal_kernel(
    heads, d_skip, xs, dxs, zgate, bmat, cmat, shifted, logs, local_in, fin, base, slope
):
    width = xs.shape[0] // heads
    block = pl.program_id(0)
    mine = pl.ds(pl.multiple_of(block * PACK, PACK), PACK)
    log_rows, shifted_rows = logs[mine, :], shifted[mine, :]
    table = jnp.concatenate([log_rows, jnp.zeros((LANES - PACK, Q), F32)], axis=0).T
    log_wide = [jnp.broadcast_to(table[:, h : h + 1], (Q, LANES)) for h in range(heads)]
    decays = [jnp.exp(wide) for wide in log_wide]
    through = fin[mine, 0:1]
    scores = across(cmat[...], bmat[...])
    causal = lax.broadcasted_iota(jnp.int32, (HALF, HALF), 0) >= lax.broadcasted_iota(
        jnp.int32, (HALF, HALF), 1
    )
    unit = (
        lax.broadcasted_iota(jnp.int32, (Q, Q), 0) == lax.broadcasted_iota(jnp.int32, (Q, Q), 1)
    ).astype(BF16)
    nothing = jnp.zeros((HALF, HALF), BF16)
    z = across(unit, zgate[...])
    gate = z * (0.5 + 0.5 * jnp.tanh(0.5 * z))
    gate_last = gate[:, 2 * LANES :]
    gates = [
        gate[:, :LANES],
        gate[:, LANES : 2 * LANES],
        jnp.concatenate([gate_last, gate_last], axis=1),
    ]
    low = lax.broadcasted_iota(jnp.int32, (Q, LANES), 1) < LANES // 2

    def weights(h):
        log_t = log_wide[h]
        log_s = shifted_rows[h : h + 1, :]
        near = scores[:HALF, :HALF] * jnp.exp(log_t[:HALF] - log_s[:, :HALF])
        far = scores[HALF:, :HALF] * jnp.exp(log_t[HALF:] - log_s[:, :HALF])
        last = scores[HALF:, HALF:] * jnp.exp(log_t[HALF:] - log_s[:, HALF:])
        top = jnp.concatenate([jnp.where(causal, near, 0.0).astype(BF16), nothing], axis=1)
        bottom = jnp.concatenate([far, jnp.where(causal, last, 0.0)], axis=1).astype(BF16)
        return [top, bottom]

    carried = across(cmat[...], local_in[0])
    factors = [through[h : h + 1, :] for h in range(heads)]
    skip = by_head([d_skip[h] for h in range(heads)], 1)
    rows = feature_rows(xs[...], dxs[...], heads, width)
    for pair in range(0, heads, 2):
        members = range(pair, min(pair + 2, heads))
        operand = jnp.concatenate([part for h, part in rows if h in members], axis=0)
        left = [piece for h in members for piece in weights(h)] + [unit]
        sums = across(jnp.concatenate(left, axis=0), operand)
        count = len(members)
        decay, factor = decays[pair], factors[pair]
        if count == 2:
            decay = jnp.where(low, decay, decays[pair + 1])
            factor = jnp.where(low, factor, factors[pair + 1])
        for i in range(count):
            tile = pair + i
            at = slice(tile * LANES, (tile + 1) * LANES)
            lanes = slice(i * LANES, (i + 1) * LANES)
            diagonal = sums[:Q, lanes]
            if count == 2:
                diagonal = jnp.where(low, diagonal, sums[Q : 2 * Q, lanes])
            plain = sums[count * Q :, lanes]
            y = diagonal + carried[:, at] * decay + plain * skip[tile]
            base[:, at] = (y * gates[pair // 2]).astype(BF16)
        at = slice(pair // 2 * LANES, (pair // 2 + 1) * LANES)
        slope[:, at] = (decay * factor * gates[pair // 2]).astype(BF16)


def gate_kernel(blocks, heads, base, slope, cmat, incoming, out):
    state = incoming[...]
    for c in range(blocks):
        here = slice(c * Q, (c + 1) * Q)
        carried = jnp.dot(cmat[here, :], state, preferred_element_type=F32)
        for i in range(heads):
            at = slice(i * LANES, (i + 1) * LANES)
            gain = slope[here, i // 2 * LANES : (i // 2 + 1) * LANES].astype(F32)
            out[here, at] = (base[here, at].astype(F32) + carried[:, at] * gain).astype(BF16)


def norm_kernel(
    heads, sources, strip, strips, total_width, gathered, gain, normed, normed_tan, held, sems
):
    half = LANES // 2
    width = heads * half
    copies = []
    for r in range(strips):
        here = slice(r * strip, (r + 1) * strip)
        main_parts, tan_parts = [], []
        for s in range(sources):
            tiles = [
                gathered[s, here, i * LANES : (i + 1) * LANES].astype(F32) for i in range(heads)
            ]
            main_parts += [tiles[0], tiles[2], tiles[4][:, :half]]
            tan_parts += [tiles[1], tiles[3], tiles[4][:, half:]]
        mains, tans = [], []
        for s in range(0, sources, 2):
            mains.append(jnp.concatenate(main_parts[3 * s : 3 * s + 6], axis=1))
            tans.append(jnp.concatenate(tan_parts[3 * s : 3 * s + 6], axis=1))
        square = sum(m * m for m in mains)
        cross = sum(m * t for m, t in zip(mains, tans))
        mean_square = jnp.sum(square, axis=1, keepdims=True) / total_width
        mean_cross = jnp.sum(cross, axis=1, keepdims=True) / total_width
        inv_rms = lax.rsqrt(mean_square + 1e-05)
        pull = inv_rms * inv_rms * inv_rms * mean_cross
        for i, (m, t) in enumerate(zip(mains, tans)):
            at = slice(i * 2 * width, (i + 1) * 2 * width)
            g = gain[:, at]
            held[0, here, at] = (g * m * inv_rms).astype(BF16)
            held[1, here, at] = (g * (t * inv_rms - m * pull)).astype(BF16)
        for k, target in enumerate((normed, normed_tan)):
            copy = pltpu.make_async_copy(held.at[k, here, :], target.at[here, :], sems.at[k, r])
            copy.start()
            copies.append(copy)
    for copy in copies:
        copy.wait()


def whole(shape):
    return pl.BlockSpec(shape, lambda *_: (0,) * len(shape))


SMEM_SPEC = pl.BlockSpec(memory_space=pltpu.SMEM)


def local(xs, dxs, zgate, bmat, cmat, dt_raw, dt_bias, a_rate, d_skip, gain, traj_ids):
    tokens, inner = xs.shape
    heads = dt_raw.shape[0]
    blocks = tokens // Q
    wide = heads * LANES
    state_rows = bmat.shape[1]
    sources = lax.axis_size("head")
    seq_size = lax.axis_size("seq")
    group = state_rows // PACK
    groups = [list(range(g, g + group)) for g in range(0, seq_size, group)]
    params = pltpu.CompilerParams(vmem_limit_bytes=60 * MIB)
    roomy = pltpu.CompilerParams(vmem_limit_bytes=32 * MIB)
    small = pltpu.CompilerParams(vmem_limit_bytes=16 * MIB)
    in_vmem = pl.BlockSpec(memory_space=pltpu.VMEM)
    in_hbm = pl.BlockSpec(memory_space=pl.ANY)
    c_plain = cmat
    xs, dxs, zgate, bmat, cmat, dt_raw = [
        pltpu.with_memory_space_constraint(array, pltpu.HBM)
        for array in (xs.T, dxs.T, zgate.T, bmat, cmat, dt_raw)
    ]

    def pinned(array):
        return pltpu.with_memory_space_constraint(array, pltpu.VMEM)

    shifted, logs, local_in, fin, send = pl.pallas_call(
        functools.partial(state_kernel, heads, blocks),
        out_shape=(
            pltpu.VMEM((blocks * PACK, Q), F32),
            pltpu.VMEM((blocks * PACK, Q), F32),
            jax.ShapeDtypeStruct((blocks, wide, state_rows), BF16),
            pltpu.VMEM((blocks * PACK, LANES), F32),
            pltpu.VMEM((state_rows, wide + LANES), BF16),
        ),
        in_specs=[in_hbm] * 7,
        out_specs=(in_vmem, in_vmem, in_hbm, in_vmem, in_vmem),
        scratch_shapes=[
            pltpu.VMEM((inner, tokens), BF16),
            pltpu.VMEM((inner, tokens), BF16),
            pltpu.VMEM((tokens, state_rows), BF16),
            pltpu.VMEM((blocks, wide, state_rows), BF16),
            pltpu.VMEM((heads, tokens), F32),
            pltpu.SMEM((heads,), F32),
            pltpu.SMEM((heads,), F32),
            pltpu.SMEM((blocks,), jnp.int32),
            pltpu.SemaphoreType.DMA((3, len(range(0, heads, 2)))),
            pltpu.SemaphoreType.DMA((len(range(0, heads, 2)),)),
            pltpu.SemaphoreType.DMA((3,)),
        ],
        compiler_params=params,
        cost_estimate=pl.CostEstimate(
            flops=300_000_000, bytes_accessed=4_000_000, transcendentals=30_000
        ),
    )(dt_bias, a_rate, traj_ids, dt_raw, xs, dxs, bmat)

    def token_block(width):
        return pl.BlockSpec((Q, width), lambda c: (c, 0))

    def feature_block(width):
        return pl.BlockSpec((width, Q), lambda c: (0, c))

    lean = (heads + 1) // 2 * LANES
    base, slope = pl.pallas_call(
        functools.partial(diagonal_kernel, heads),
        grid=(blocks,),
        out_shape=(
            pltpu.VMEM((tokens, wide), BF16),
            pltpu.VMEM((tokens, lean), BF16),
        ),
        in_specs=[
            SMEM_SPEC,
            feature_block(inner),
            feature_block(inner),
            feature_block(inner),
            token_block(state_rows),
            token_block(state_rows),
            in_vmem,
            in_vmem,
            pl.BlockSpec((1, wide, state_rows), lambda c: (c, 0, 0)),
            in_vmem,
        ],
        out_specs=(token_block(wide), token_block(lean)),
        compiler_params=roomy,
        cost_estimate=pl.CostEstimate(
            flops=2_000_000_000, bytes_accessed=16_000_000, transcendentals=2_000_000
        ),
    )(
        d_skip,
        xs,
        dxs,
        zgate,
        bmat,
        cmat,
        pinned(shifted),
        pinned(logs),
        pltpu.with_memory_space_constraint(local_in, pltpu.HBM),
        pinned(fin),
    )

    got = lax.all_to_all(
        send, "seq", split_axis=0, concat_axis=0, tiled=True, axis_index_groups=groups
    )
    back = pl.pallas_call(
        functools.partial(scan_kernel, heads, group),
        out_shape=jax.ShapeDtypeStruct((state_rows, wide), BF16),
        in_specs=[in_vmem, in_hbm],
        scratch_shapes=[pltpu.VMEM((state_rows, wide), F32)],
        compiler_params=small,
    )(got, pinned(slope))
    incoming = lax.all_to_all(
        back, "seq", split_axis=0, concat_axis=0, tiled=True, axis_index_groups=groups
    )
    gated = pl.pallas_call(
        functools.partial(gate_kernel, blocks, heads),
        out_shape=jax.ShapeDtypeStruct((tokens, wide), BF16),
        in_specs=[in_vmem] * 4,
        compiler_params=small,
        cost_estimate=pl.CostEstimate(
            flops=260_000_000, bytes_accessed=6_000_000, transcendentals=0
        ),
    )(
        pinned(base),
        pinned(slope),
        pinned(c_plain),
        incoming,
    )

    gathered = lax.all_to_all(gated, "head", split_axis=0, concat_axis=0, tiled=True)
    mine = tokens // sources
    strip = 16
    strips = mine // strip
    total = inner * sources
    return pl.pallas_call(
        functools.partial(norm_kernel, heads, sources, strip, strips, float(total)),
        out_shape=(
            jax.ShapeDtypeStruct((mine, total), BF16),
            jax.ShapeDtypeStruct((mine, total), BF16),
        ),
        in_specs=[in_vmem] * 2,
        out_specs=(in_hbm, in_hbm),
        scratch_shapes=[
            pltpu.VMEM((2, mine, total), BF16),
            pltpu.SemaphoreType.DMA((2, strips)),
        ],
        compiler_params=small,
    )(gathered.reshape(sources, mine, wide), gain.reshape(1, total))


def solution(mesh):
    placed = (
        P("seq", "head"),
        P("seq", "head"),
        P("seq", "head"),
        P("seq", None),
        P("seq", None),
        P("head", "seq"),
        P("head"),
        P("head"),
        P("head"),
        P(),
        P("seq"),
    )
    return jax.shard_map(
        local,
        mesh=mesh,
        in_specs=placed,
        out_specs=(P(("seq", "head"), None), P(("seq", "head"), None)),
        check_vma=False,
    )
```

```python
import functools

import jax
import jax.numpy as jnp
from jax import lax
from jax.experimental import pallas as pl
from jax.experimental.pallas import tpu as pltpu
from jax.sharding import PartitionSpec as P

Q = 256
HALF = 128
LANES = 128
PACK = 8
MIB = 1024 * 1024
F32 = jnp.float32
BF16 = jnp.bfloat16


def column_of(values):
    place = lax.broadcasted_iota(jnp.int32, (PACK, 1), 0)
    column = jnp.zeros((PACK, 1), F32)
    for h, value in enumerate(values):
        column = jnp.where(place == h, value, column)
    return column


def by_head(per_head, rows):
    low = lax.broadcasted_iota(jnp.int32, (rows, LANES), 1) < LANES // 2
    first = jnp.where(low, per_head[0], per_head[1])
    second = jnp.where(low, per_head[2], per_head[3])
    last = jnp.broadcast_to(per_head[4], (rows, LANES))
    return [first, first, second, second, last]


def feature_rows(main, tan, heads, width):
    order = []
    for pair in range(0, heads, 2):
        for array in (main, tan):
            for h in range(pair, min(pair + 2, heads)):
                order.append((h, array[h * width : (h + 1) * width, :]))
    return order


def split_bf16(x, parts):
    pieces = []
    for _ in range(parts):
        piece = x.astype(BF16)
        pieces.append(piece)
        x = x - piece.astype(F32)
    return pieces


def across(left, right):
    return lax.dot_general(left, right, (((1,), (1,)), ((), ())), preferred_element_type=F32)


def state_kernel(
    heads,
    blocks,
    bias_hbm,
    rate_hbm,
    traj_hbm,
    dt_hbm,
    xs_hbm,
    dxs_hbm,
    bmat_hbm,
    shifted_out,
    logs_out,
    local_out,
    fin,
    send,
    xs,
    dxs,
    bmat,
    local_in,
    dt_raw,
    dt_bias,
    a_rate,
    traj,
    sems,
    out_sems,
    small_sems,
):
    width = xs.shape[0] // heads
    chunks = [slice(h * width, min(h + 2, heads) * width) for h in range(0, heads, 2)]
    b_copy = pltpu.make_async_copy(bmat_hbm, bmat, sems.at[2, 0])
    dt_copy = pltpu.make_async_copy(dt_hbm, dt_raw, sems.at[2, 1])
    dt_copy.start()
    head_rows = chunks[0].stop
    parts = [pl.ds(0, head_rows), pl.ds(head_rows, xs.shape[0] - head_rows)]
    copies = [
        [
            pltpu.make_async_copy(xs_hbm.at[part, :], xs.at[part, :], sems.at[0, i]),
            pltpu.make_async_copy(dxs_hbm.at[part, :], dxs.at[part, :], sems.at[1, i]),
        ]
        for i, part in enumerate(parts)
    ] + [[] for _ in chunks[2:]]
    for copy in copies[0] + [b_copy] + copies[1]:
        copy.start()
    small_copies = [
        pltpu.make_async_copy(source, target, small_sems.at[i])
        for i, (source, target) in enumerate(
            ((bias_hbm, dt_bias), (rate_hbm, a_rate), (traj_hbm, traj))
        )
    ]
    for copy in small_copies:
        copy.start()
    for copy in small_copies:
        copy.wait()
    bias = column_of([dt_bias[h] for h in range(heads)])
    rate = column_of([a_rate[h] for h in range(heads)])
    dt_copy.wait()
    raw = jnp.concatenate([dt_raw[...], jnp.zeros((PACK - heads, blocks * Q), F32)], axis=0)
    pre = jnp.concatenate([raw[:, c * Q : (c + 1) * Q] for c in range(blocks)], axis=0)
    pre = pre + jnp.concatenate([bias] * blocks, axis=0)
    step = jnp.maximum(pre, 0.0) + jnp.log1p(jnp.exp(-jnp.abs(pre)))
    upper = (
        lax.broadcasted_iota(jnp.int32, (Q, Q), 0) <= lax.broadcasted_iota(jnp.int32, (Q, Q), 1)
    ).astype(BF16)
    logs = jnp.zeros((blocks * PACK, Q), F32)
    for piece in split_bf16(-(step * jnp.concatenate([rate] * blocks, axis=0)), 3)[::-1]:
        logs = logs + jnp.dot(piece, upper, preferred_element_type=F32)
    shifted = logs - jnp.log(step)
    shifted_out[...] = shifted
    logs_out[...] = logs
    ends = logs[:, Q - 1 : Q]
    weight_in = jnp.exp(ends - shifted)
    end_decay = jnp.exp(ends)

    factor = jnp.ones((PACK, 1), F32)
    keeps = [None]
    for c in range(blocks):
        if c > 0:
            keeps.append(jnp.where(traj[c] == traj[c - 1], 1.0, 0.0))
            factor = factor * keeps[c]
        fin[c * PACK : (c + 1) * PACK, :] = jnp.broadcast_to(factor, (PACK, LANES))
        factor = factor * end_decay[c * PACK : (c + 1) * PACK, :]
    copies_out = []
    b_copy.wait()
    for i, at in enumerate(chunks):
        for copy in copies[i]:
            copy.wait()
        members = [h for h in range(2 * i, min(2 * i + 2, heads))] * 2
        place = slice(2 * at.start, 2 * at.stop)
        state = jnp.zeros((len(members) * width, LANES), F32)
        for c in range(blocks):
            here = slice(c * Q, (c + 1) * Q)
            if c > 0:
                state = state * keeps[c]
            local_in[c, place, :] = state.astype(BF16)
            both = jnp.concatenate([xs[at, here], dxs[at, here]], axis=0).astype(F32)
            scale = jnp.concatenate(
                [
                    jnp.broadcast_to(
                        weight_in[c * PACK + h : c * PACK + h + 1, :], (width, Q)
                    )
                    for h in members
                ],
                axis=0,
            )
            gained = jnp.dot(
                (both * scale).astype(BF16), bmat[here, :], preferred_element_type=F32
            )
            decay = jnp.concatenate(
                [
                    jnp.broadcast_to(
                        end_decay[c * PACK + h : c * PACK + h + 1, :], (width, LANES)
                    )
                    for h in members
                ],
                axis=0,
            )
            state = state * decay + gained
        rows = pl.ds(place.start, place.stop - place.start)
        leaving = pltpu.make_async_copy(
            local_in.at[:, rows, :], local_out.at[:, rows, :], out_sems.at[i]
        )
        leaving.start()
        copies_out.append(leaving)
        send[:, place] = state.T.astype(BF16)
    lane = lax.broadcasted_iota(jnp.int32, (1, LANES), 1)
    notes = jnp.zeros((1, LANES), F32)
    for h in range(heads):
        rest = factor[h : h + 1, :]
        for k in range(3):
            piece = rest.astype(BF16).astype(F32)
            notes = jnp.where(lane == k * heads + h, piece, notes)
            rest = rest - piece
    notes = jnp.where(lane == 3 * heads, traj[0].astype(F32), notes)
    notes = jnp.where(lane == 3 * heads + 1, traj[blocks - 1].astype(F32), notes)
    send[:, heads * LANES :] = jnp.broadcast_to(notes, (LANES, LANES)).astype(BF16)
    for leaving in copies_out:
        leaving.wait()


def scan_kernel(heads, count, got, _, back, hold):
    width = heads * LANES
    everything = got[...].astype(F32)
    carried = jnp.zeros((PACK, width), F32)
    last_id = None
    for s in range(count):
        at = slice(s * PACK, (s + 1) * PACK)
        notes = everything[at, width:]
        factor = []
        for h in range(heads):
            total = notes[:, h : h + 1]
            for k in range(1, 3):
                total = total + notes[:, k * heads + h : k * heads + h + 1]
            factor.append(total)
        first_id = notes[:, 3 * heads : 3 * heads + 1]
        if s > 0:
            carried = jnp.where(first_id == last_id, carried, 0.0)
        hold[at, :] = carried
        last_id = notes[:, 3 * heads + 1 : 3 * heads + 2]
        carried = jnp.concatenate(by_head(factor, PACK), axis=1) * carried + everything[at, :width]
    back[...] = hold[...].astype(BF16)


def diagonal_kernel(
    heads, d_skip, xs, dxs, zgate, bmat, cmat, shifted, logs, local_in, fin, base, slope
):
    width = xs.shape[0] // heads
    block = pl.program_id(0)
    mine = pl.ds(pl.multiple_of(block * PACK, PACK), PACK)
    log_rows, shifted_rows = logs[mine, :], shifted[mine, :]
    table = jnp.concatenate([log_rows, jnp.zeros((LANES - PACK, Q), F32)], axis=0).T
    log_wide = [jnp.broadcast_to(table[:, h : h + 1], (Q, LANES)) for h in range(heads)]
    decays = [jnp.exp(wide) for wide in log_wide]
    through = fin[mine, 0:1]
    scores = across(cmat[...], bmat[...])
    causal = lax.broadcasted_iota(jnp.int32, (HALF, HALF), 0) >= lax.broadcasted_iota(
        jnp.int32, (HALF, HALF), 1
    )
    nothing = jnp.zeros((HALF, HALF), BF16)
    z = zgate[...].T.astype(F32)
    gate = z * (0.5 + 0.5 * jnp.tanh(0.5 * z))
    gate_last = gate[:, 2 * LANES :]
    gates = [
        gate[:, :LANES],
        gate[:, LANES : 2 * LANES],
        jnp.concatenate([gate_last, gate_last], axis=1),
    ]
    low = lax.broadcasted_iota(jnp.int32, (Q, LANES), 1) < LANES // 2

    def weights(h):
        log_t = log_wide[h]
        log_s = shifted_rows[h : h + 1, :]
        near = scores[:HALF, :HALF] * jnp.exp(log_t[:HALF] - log_s[:, :HALF])
        far = scores[HALF:, :HALF] * jnp.exp(log_t[HALF:] - log_s[:, :HALF])
        last = scores[HALF:, HALF:] * jnp.exp(log_t[HALF:] - log_s[:, HALF:])
        top = jnp.concatenate([jnp.where(causal, near, 0.0).astype(BF16), nothing], axis=1)
        bottom = jnp.concatenate([far, jnp.where(causal, last, 0.0)], axis=1).astype(BF16)
        return [top, bottom]

    carried = across(cmat[...], local_in[0])
    factors = [through[h : h + 1, :] for h in range(heads)]
    skip = by_head([d_skip[h] for h in range(heads)], 1)
    rows = feature_rows(xs[...], dxs[...], heads, width)
    for pair in range(0, heads, 2):
        members = range(pair, min(pair + 2, heads))
        operand = jnp.concatenate([part for h, part in rows if h in members], axis=0)
        left = [piece for h in members for piece in weights(h)]
        sums = across(jnp.concatenate(left, axis=0), operand)
        turned = operand.T.astype(F32)
        count = len(members)
        decay, factor = decays[pair], factors[pair]
        if count == 2:
            decay = jnp.where(low, decay, decays[pair + 1])
            factor = jnp.where(low, factor, factors[pair + 1])
        for i in range(count):
            tile = pair + i
            at = slice(tile * LANES, (tile + 1) * LANES)
            lanes = slice(i * LANES, (i + 1) * LANES)
            diagonal = sums[:Q, lanes]
            if count == 2:
                diagonal = jnp.where(low, diagonal, sums[Q : 2 * Q, lanes])
            plain = turned[:, lanes]
            y = diagonal + carried[:, at] * decay + plain * skip[tile]
            base[:, at] = (y * gates[pair // 2]).astype(BF16)
        at = slice(pair // 2 * LANES, (pair // 2 + 1) * LANES)
        slope[:, at] = (decay * factor * gates[pair // 2]).astype(BF16)


def gate_kernel(blocks, heads, base, slope, cmat, incoming, out):
    state = incoming[...]
    for c in range(blocks):
        here = slice(c * Q, (c + 1) * Q)
        carried = jnp.dot(cmat[here, :], state, preferred_element_type=F32)
        for i in range(heads):
            at = slice(i * LANES, (i + 1) * LANES)
            gain = slope[here, i // 2 * LANES : (i // 2 + 1) * LANES].astype(F32)
            out[here, at] = (base[here, at].astype(F32) + carried[:, at] * gain).astype(BF16)


def norm_kernel(
    heads, sources, strip, strips, total_width, gathered, gain, normed, normed_tan, held, sems
):
    half = LANES // 2
    width = heads * half
    copies = []
    for r in range(strips):
        here = slice(r * strip, (r + 1) * strip)
        main_parts, tan_parts = [], []
        for s in range(sources):
            tiles = [
                gathered[s, here, i * LANES : (i + 1) * LANES].astype(F32) for i in range(heads)
            ]
            main_parts += [tiles[0], tiles[2], tiles[4][:, :half]]
            tan_parts += [tiles[1], tiles[3], tiles[4][:, half:]]
        mains, tans = [], []
        for s in range(0, sources, 2):
            mains.append(jnp.concatenate(main_parts[3 * s : 3 * s + 6], axis=1))
            tans.append(jnp.concatenate(tan_parts[3 * s : 3 * s + 6], axis=1))
        square = sum(m * m for m in mains)
        cross = sum(m * t for m, t in zip(mains, tans))
        mean_square = jnp.sum(square, axis=1, keepdims=True) / total_width
        mean_cross = jnp.sum(cross, axis=1, keepdims=True) / total_width
        inv_rms = lax.rsqrt(mean_square + 1e-05)
        pull = inv_rms * inv_rms * inv_rms * mean_cross
        for i, (m, t) in enumerate(zip(mains, tans)):
            at = slice(i * 2 * width, (i + 1) * 2 * width)
            g = gain[:, at]
            held[0, here, at] = (g * m * inv_rms).astype(BF16)
            held[1, here, at] = (g * (t * inv_rms - m * pull)).astype(BF16)
        for k, target in enumerate((normed, normed_tan)):
            copy = pltpu.make_async_copy(held.at[k, here, :], target.at[here, :], sems.at[k, r])
            copy.start()
            copies.append(copy)
    for copy in copies:
        copy.wait()


def whole(shape):
    return pl.BlockSpec(shape, lambda *_: (0,) * len(shape))


SMEM_SPEC = pl.BlockSpec(memory_space=pltpu.SMEM)


def local(xs, dxs, zgate, bmat, cmat, dt_raw, dt_bias, a_rate, d_skip, gain, traj_ids):
    tokens, inner = xs.shape
    heads = dt_raw.shape[0]
    blocks = tokens // Q
    wide = heads * LANES
    state_rows = bmat.shape[1]
    sources = lax.axis_size("head")
    seq_size = lax.axis_size("seq")
    group = state_rows // PACK
    groups = [list(range(g, g + group)) for g in range(0, seq_size, group)]
    params = pltpu.CompilerParams(vmem_limit_bytes=60 * MIB)
    roomy = pltpu.CompilerParams(vmem_limit_bytes=32 * MIB)
    small = pltpu.CompilerParams(vmem_limit_bytes=16 * MIB)
    in_vmem = pl.BlockSpec(memory_space=pltpu.VMEM)
    in_hbm = pl.BlockSpec(memory_space=pl.ANY)
    c_plain = cmat
    xs, dxs, zgate, bmat, cmat, dt_raw = [
        pltpu.with_memory_space_constraint(array, pltpu.HBM)
        for array in (xs.T, dxs.T, zgate.T, bmat, cmat, dt_raw)
    ]

    def pinned(array):
        return pltpu.with_memory_space_constraint(array, pltpu.VMEM)

    shifted, logs, local_in, fin, send = pl.pallas_call(
        functools.partial(state_kernel, heads, blocks),
        out_shape=(
            pltpu.VMEM((blocks * PACK, Q), F32),
            pltpu.VMEM((blocks * PACK, Q), F32),
            jax.ShapeDtypeStruct((blocks, wide, state_rows), BF16),
            pltpu.VMEM((blocks * PACK, LANES), F32),
            pltpu.VMEM((state_rows, wide + LANES), BF16),
        ),
        in_specs=[in_hbm] * 7,
        out_specs=(in_vmem, in_vmem, in_hbm, in_vmem, in_vmem),
        scratch_shapes=[
            pltpu.VMEM((inner, tokens), BF16),
            pltpu.VMEM((inner, tokens), BF16),
            pltpu.VMEM((tokens, state_rows), BF16),
            pltpu.VMEM((blocks, wide, state_rows), BF16),
            pltpu.VMEM((heads, tokens), F32),
            pltpu.SMEM((heads,), F32),
            pltpu.SMEM((heads,), F32),
            pltpu.SMEM((blocks,), jnp.int32),
            pltpu.SemaphoreType.DMA((3, len(range(0, heads, 2)))),
            pltpu.SemaphoreType.DMA((len(range(0, heads, 2)),)),
            pltpu.SemaphoreType.DMA((3,)),
        ],
        compiler_params=params,
        cost_estimate=pl.CostEstimate(
            flops=300_000_000, bytes_accessed=4_000_000, transcendentals=30_000
        ),
    )(dt_bias, a_rate, traj_ids, dt_raw, xs, dxs, bmat)

    def token_block(width):
        return pl.BlockSpec((Q, width), lambda c: (c, 0))

    def feature_block(width):
        return pl.BlockSpec((width, Q), lambda c: (0, c))

    lean = (heads + 1) // 2 * LANES
    base, slope = pl.pallas_call(
        functools.partial(diagonal_kernel, heads),
        grid=(blocks,),
        out_shape=(
            pltpu.VMEM((tokens, wide), BF16),
            pltpu.VMEM((tokens, lean), BF16),
        ),
        in_specs=[
            SMEM_SPEC,
            feature_block(inner),
            feature_block(inner),
            feature_block(inner),
            token_block(state_rows),
            token_block(state_rows),
            in_vmem,
            in_vmem,
            pl.BlockSpec((1, wide, state_rows), lambda c: (c, 0, 0)),
            in_vmem,
        ],
        out_specs=(token_block(wide), token_block(lean)),
        compiler_params=roomy,
        cost_estimate=pl.CostEstimate(
            flops=2_000_000_000, bytes_accessed=16_000_000, transcendentals=2_000_000
        ),
    )(
        d_skip,
        xs,
        dxs,
        zgate,
        bmat,
        cmat,
        pinned(shifted),
        pinned(logs),
        pltpu.with_memory_space_constraint(local_in, pltpu.HBM),
        pinned(fin),
    )

    got = lax.all_to_all(
        send, "seq", split_axis=0, concat_axis=0, tiled=True, axis_index_groups=groups
    )
    back = pl.pallas_call(
        functools.partial(scan_kernel, heads, group),
        out_shape=jax.ShapeDtypeStruct((state_rows, wide), BF16),
        in_specs=[in_vmem, in_hbm],
        scratch_shapes=[pltpu.VMEM((state_rows, wide), F32)],
        compiler_params=small,
    )(got, pinned(slope))
    incoming = lax.all_to_all(
        back, "seq", split_axis=0, concat_axis=0, tiled=True, axis_index_groups=groups
    )
    gated = pl.pallas_call(
        functools.partial(gate_kernel, blocks, heads),
        out_shape=jax.ShapeDtypeStruct((tokens, wide), BF16),
        in_specs=[in_vmem] * 4,
        compiler_params=small,
        cost_estimate=pl.CostEstimate(
            flops=260_000_000, bytes_accessed=6_000_000, transcendentals=0
        ),
    )(
        pinned(base),
        pinned(slope),
        pinned(c_plain),
        incoming,
    )

    gathered = lax.all_to_all(gated, "head", split_axis=0, concat_axis=0, tiled=True)
    mine = tokens // sources
    strip = 32
    strips = mine // strip
    total = inner * sources
    return pl.pallas_call(
        functools.partial(norm_kernel, heads, sources, strip, strips, float(total)),
        out_shape=(
            jax.ShapeDtypeStruct((mine, total), BF16),
            jax.ShapeDtypeStruct((mine, total), BF16),
        ),
        in_specs=[in_vmem] * 2,
        out_specs=(in_hbm, in_hbm),
        scratch_shapes=[
            pltpu.VMEM((2, mine, total), BF16),
            pltpu.SemaphoreType.DMA((2, strips)),
        ],
        compiler_params=small,
    )(gathered.reshape(sources, mine, wide), gain.reshape(1, total))


def solution(mesh):
    placed = (
        P("seq", "head"),
        P("seq", "head"),
        P("seq", "head"),
        P("seq", None),
        P("seq", None),
        P("head", "seq"),
        P("head"),
        P("head"),
        P("head"),
        P(),
        P("seq"),
    )
    return jax.shard_map(
        local,
        mesh=mesh,
        in_specs=placed,
        out_specs=(P(("seq", "head"), None), P(("seq", "head"), None)),
        check_vma=False,
    )
```
